128 devices in a mesh: ka: 32 (over y, z, core), gz: 4 (over x).
Axes of the slice: x: 4, y: 4, z: 4, core: 2. Of those that a mesh axis runs over, the one named last changes fastest.
Arguments:
- fields: float32 [32, 2, 32, 3, 25600], P('ka', None, None, None, 'gz'), may hold values from -0.25 to 0.25
- bvectors: float32 [2, 3], replicated, may hold values from -0.5 to 0.5
- gshift: int32 [32, 2, 3], replicated, may hold values from -1 to 1
Outputs:
- intersections: float32 [32, 4, 2, 32, 32], P('ka')
The draws below stay inside these ranges and needn't reach their ends.
All inputs are finite; a program needn't handle non-finite values.
Results may differ from the reference program's by a relative error of at most 0.0003.
Values sent between devices are 32-bit elements; how exact they have to be, the bound alone decides.
A program may use at most 128 MiB of HBM per device.

```python
import math
import jax
import jax.numpy as jnp
from jax import lax

BANDS = 32
GX = 40
GY = 40
KX = 4
NZ = 16
CELLS = 25600
K = 32


def place_ends(entries, rng, low, largest):
    extent = entries.shape
    index_at = [jax.random.randint(jax.random.fold_in(rng, axis), (), 0, extent[axis]) for axis in range(len(extent))]
    entries = entries.at[tuple(index_at)].set(low)
    longest = extent.index(max(extent))
    index_at[longest] = (index_at[longest] + 1) % extent[longest]
    return entries.at[tuple(index_at)].set(largest)


def levels(key, dims, cuts, low, top_value):
    gain, own = 1.0, jax.random.fold_in(key, 6)
    for axis_at, shards_of in cuts:
        steps = jnp.exp(jax.random.uniform(jax.random.fold_in(own, axis_at), (shards_of,), jnp.float32, low / len(cuts), top_value / len(cuts)))
        gain = gain * jnp.repeat(steps, dims[axis_at] // shards_of).reshape([-1 if axis == axis_at else 1 for axis in range(len(dims))])
    return gain


def centred(rng, dims, spread, bound, pieces=(), kind=jnp.bfloat16):
    result = jax.random.normal(rng, dims, jnp.float32) * spread
    if len(pieces) > 0:
        result = levels(rng, dims, pieces, -0.22, 0.18) * result
    return jnp.clip(result, min=-bound, max=bound).astype(kind)


def setup_inputs(seed: int = 0) -> dict:
    key_of = jax.random.split(jax.random.key(seed), 4)
    return {
        "fields": centred(key_of[0], (K, 2, BANDS, 3, CELLS), (GY * NZ) ** -0.5, 0.25, ((0, 32), (4, 4)), jnp.float32),
        "bvectors": jnp.clip(jax.random.uniform(key_of[1], (2, 3), jnp.float32, -0.5, 0.5), -0.5, 0.5),
        "gshift": place_ends(jax.random.randint(key_of[2], (K, 2, 3), -1, 2), jax.random.fold_in(key_of[2], 1), -1, 1).astype(jnp.int32),
    }


two_pi = 2.0 * math.pi


def phase_angle(q_vector, xcoord, ycoord, zcoord, x_extent, y_extent, z_extent):
    return -two_pi * (q_vector[0] * xcoord / x_extent + q_vector[1] * ycoord / y_extent + q_vector[2] * zcoord / z_extent)


def intersection(left_field, right_field, angles):
    cosine_part = jnp.cos(angles)
    sine_part = jnp.sin(angles)
    r_real = right_field[0]
    r_imag = right_field[1]
    w_real = cosine_part * r_real - sine_part * r_imag
    w_imag = sine_part * r_real + cosine_part * r_imag
    band_count = left_field.shape[1]
    left_rows = jnp.concatenate([left_field[0].reshape(band_count, -1), left_field[1].reshape(band_count, -1)], axis=1)
    upper_rows = jnp.concatenate([w_real.reshape(band_count, -1), w_imag.reshape(band_count, -1)], axis=1)
    lower_rows = jnp.concatenate([w_imag.reshape(band_count, -1), -w_real.reshape(band_count, -1)], axis=1)
    right_rows = jnp.concatenate([upper_rows, lower_rows], axis=0)
    product = lax.dot_general(left_rows, right_rows, (((1,), (1,)), ((), ())), precision=lax.Precision.HIGHEST, preferred_element_type=jnp.float32)
    return jnp.stack([product[:, :band_count], product[:, band_count:]])


def reference(fields, bvectors, gshift):
    kpoint_count = fields.shape[0]
    cell_total = fields.shape[-1]
    cell_index = jnp.arange(cell_total, dtype=jnp.int32)
    xcoord = (cell_index % GX).astype(jnp.float32)
    ycoord = ((cell_index // GX) % GY).astype(jnp.float32)
    zcoord = (cell_index // (GX * GY)).astype(jnp.float32)
    shifts_float = gshift.astype(jnp.float32)

    def one_point(kpoint):
        plus_x = (kpoint + 1) % kpoint_count
        minus_x = (kpoint - 1 + kpoint_count) % kpoint_count
        plus_y = (kpoint + KX) % kpoint_count
        minus_y = (kpoint - KX + kpoint_count) % kpoint_count
        local_field = fields[kpoint]
        q_plus_x = bvectors[0] + shifts_float[kpoint, 0]
        q_minus_x = -(bvectors[0] + shifts_float[minus_x, 0])
        q_plus_y = bvectors[1] + shifts_float[kpoint, 1]
        q_minus_y = -(bvectors[1] + shifts_float[minus_y, 1])
        blocks = []
        for partner, q_vector in ((plus_x, q_plus_x), (minus_x, q_minus_x), (plus_y, q_plus_y), (minus_y, q_minus_y)):
            angles = phase_angle(q_vector, xcoord, ycoord, zcoord, GX, GY, NZ)
            blocks.append(intersection(local_field, fields[partner], angles))
        return jnp.stack(blocks)

    return lax.map(one_point, jnp.arange(kpoint_count, dtype=jnp.int32))
```

```python
import math

import jax
import jax.numpy as jnp
from jax import lax
from jax.experimental import pallas as pl
from jax.experimental.pallas import tpu as pltpu
from jax.sharding import PartitionSpec as P

GX = 40
GY = 40
NZ = 16
ROW = 8
ROWS = 4
SLOTS = 12
TILES = 6
HALF = 3
LANES = 128
MESH = pl.DeviceIdType.MESH
TWO_PI = 2.0 * math.pi


def split(value):
    high = value.astype(jnp.bfloat16)
    low = (value - high.astype(jnp.float32)).astype(jnp.bfloat16)
    return high, low


def contract(left, right):
    return lax.dot_general(
        left, right, (((1,), (1,)), ((), ())), preferred_element_type=jnp.float32
    )


def kernel(
    bvec_ref, gshift_ref, field_ref, out_ref,
    buf, xbuf, phase, acc, stage, reduced, total, gathered,
    send_sem, recv_sem, xsend_sem, xrecv_sem, fsend_sem, xfsend_sem,
    rsend_sem, rrecv_sem, gsend_sem, grecv_sem, rows_sem,
):
    me = lax.axis_index("ka")
    gx = lax.axis_index("gz")
    row = me // ROW
    own = me % ROW
    zpos = own // 2
    core = own % 2
    row_up = (row + 1) % ROWS
    row_down = (row + ROWS - 1) % ROWS

    def at(r, j):
        return {"ka": r * ROW + j}

    def peer(dz, dc):
        return ((zpos + dz) % 4) * 2 + (core + dc) % 2

    peers = [peer(2, 0), peer(2, 1), peer(1, 0), peer(3, 0), peer(1, 1), peer(3, 1), peer(0, 1)]

    barrier = pltpu.get_barrier_semaphore()
    for p in peers:
        pl.semaphore_signal(barrier, inc=1, device_id=at(row, p), device_id_type=MESH)
    for r in (row_up, row_down):
        pl.semaphore_signal(barrier, inc=1, device_id=at(r, own), device_id_type=MESH)
    for dx in (1, 2, 3):
        pl.semaphore_signal(barrier, inc=1, device_id={"gz": (gx + dx) % 4}, device_id_type=MESH)
    pl.semaphore_wait(barrier, 12)

    def extra_source(p):
        comp = jnp.minimum(p // 2, 2)
        start = pl.multiple_of((ROW * TILES + p % 2) * LANES, LANES)
        return field_ref.at[:, comp, :, pl.ds(start, LANES)]

    def tile_source(p, t):
        start = pl.multiple_of((p * TILES + t) * LANES, LANES)
        return field_ref.at[:, :, :, pl.ds(start, LANES)]

    for p in peers:
        pltpu.make_async_remote_copy(
            src_ref=extra_source(p), dst_ref=xbuf.at[own],
            send_sem=xsend_sem, recv_sem=xrecv_sem.at[own // 4],
            device_id=at(row, p), device_id_type=MESH,
        ).start()
    pltpu.make_async_copy(extra_source(own), xbuf.at[own], xrecv_sem.at[own // 4]).start()

    def send_tile(n, carry):
        t = (n + HALF * (zpos // 2)) % TILES
        shift = t // HALF
        slot = t * SLOTS + own + 4 * shift
        group = own // 4 + shift
        for p in peers:
            pltpu.make_async_remote_copy(
                src_ref=tile_source(p, t), dst_ref=buf.at[slot],
                send_sem=send_sem.at[t], recv_sem=recv_sem.at[t, group],
                device_id=at(row, p), device_id_type=MESH,
            ).start()
        pltpu.make_async_copy(tile_source(own, t), buf.at[slot], recv_sem.at[t, group]).start()
        return carry

    lax.fori_loop(0, TILES, send_tile, 0)

    for r in (row_up, row_down):
        pl.semaphore_signal(rows_sem, inc=1, device_id=at(r, own), device_id_type=MESH)

    row_id = lax.broadcasted_iota(jnp.int32, (16, LANES), 0)
    lane = lax.broadcasted_iota(jnp.int32, (16, LANES), 1).astype(jnp.float32)

    def q_rows(h):
        parts = []
        for a in range(3):
            q = jnp.zeros((16, LANES), jnp.float32)
            for d in range(2):
                for i in range(8):
                    k = (row * ROW + i - 4 * h + 32) % 32
                    value = bvec_ref[d, a] + gshift_ref[a, d, k].astype(jnp.float32)
                    q = jnp.where(row_id == d * 8 + i, value, q)
            parts.append(q)
        return parts

    def write_phase(index, q, start, keep):
        cell = lane + start.astype(jnp.float32)
        line = jnp.floor((cell + 0.5) * (1.0 / GX))
        plane = jnp.floor((cell + 0.5) * (1.0 / (GX * GY)))
        xc = cell - GX * line
        yc = line - GY * plane
        zc = plane + (gx * 4).astype(jnp.float32)
        theta = -TWO_PI * (q[0] * xc / GX + q[1] * yc / GY + q[2] * zc / NZ)
        phase[index, 0] = jnp.cos(theta) * keep
        phase[index, 1] = jnp.sin(theta) * keep

    for h in range(2):
        q = q_rows(h)

        def tile_phase(n, carry):
            write_phase(h * HALF + n, q, (own * TILES + h * HALF + n) * LANES, 1.0)
            return carry

        lax.fori_loop(0, HALF, tile_phase, 0)
        if h == 0:
            keep = (own < 6).astype(jnp.float32)
            write_phase(TILES, q, (ROW * TILES + own % 2) * LANES, keep)

    acc[...] = jnp.zeros_like(acc)

    def wait_tile(t, group):
        block = buf.at[pl.ds(t * SLOTS + 4 * group, 4)]
        pltpu.make_async_copy(block, block, recv_sem.at[t, group]).wait()

    def wait_extra(group):
        block = xbuf.at[pl.ds(4 * group, 4)]
        pltpu.make_async_copy(block, block, xrecv_sem.at[group]).wait()

    def forward(src, dst, ssem, rsem, target):
        return pltpu.make_async_remote_copy(
            src_ref=src, dst_ref=dst, send_sem=ssem, recv_sem=rsem,
            device_id=at(target, own), device_id_type=MESH,
        )

    def forward_extra():
        return forward(xbuf.at[pl.ds(0, 4)], xbuf.at[pl.ds(8, 4)], xfsend_sem, xrecv_sem.at[2], row_down)

    def forward_low(t):
        return forward(
            buf.at[pl.ds(t * SLOTS, 4)], buf.at[pl.ds(t * SLOTS + 8, 4)],
            fsend_sem.at[t], recv_sem.at[t, 2], row_down,
        )

    def forward_high(t):
        return forward(
            buf.at[pl.ds(t * SLOTS + 8, 4)], buf.at[pl.ds(t * SLOTS, 4)],
            fsend_sem.at[t], recv_sem.at[t, 0], row_up,
        )

    wait_extra(0)
    forward_extra().start()

    def forward_tiles(n, carry):
        wait_tile(n, 0)
        forward_low(n).start()
        wait_tile(n + HALF, 2)
        forward_high(n + HALF).start()
        return carry

    lax.fori_loop(0, HALF, forward_tiles, 0)

    def pair_products(left, rights):
        left_high, left_low = split(left)
        right_high, right_low = split(jnp.concatenate(rights, axis=0))
        return (
            contract(left_high, right_high)
            + contract(left_high, right_low)
            + contract(left_low, right_high)
        )

    def rotate(real, imag, index, d, i, comps):
        c = phase[index, 0, pl.ds(d * 8 + i, 1), :]
        s = phase[index, 1, pl.ds(d * 8 + i, 1), :]
        c = jnp.concatenate([jnp.broadcast_to(c, (32, LANES))] * comps, axis=1)
        s = jnp.concatenate([jnp.broadcast_to(s, (32, LANES))] * comps, axis=1)
        return [c * real - s * imag, s * real + c * imag]

    def extra_step(i, carry):
        left = xbuf[i].reshape(64, LANES)
        rights = []
        for d, offset in enumerate((1, 4)):
            rights += rotate(xbuf[i + offset, 0], xbuf[i + offset, 1], TILES, d, i, 1)
        acc[i + 4] += pair_products(left, rights)
        return carry

    def wide(slot, part):
        return jnp.concatenate([buf[slot, part, comp] for comp in range(3)], axis=1)

    def tile_step(t, shift, i):
        base = t * SLOTS + i
        left = jnp.concatenate([wide(base, 0), wide(base, 1)], axis=0)
        rights = []
        for d, offset in enumerate((1, 4)):
            rights += rotate(wide(base + offset, 0), wide(base + offset, 1), t, d, i, 3)
        acc[i + shift] += pair_products(left, rights)

    wait_extra(1)
    wait_extra(2)
    lax.fori_loop(0, 8, extra_step, 0)

    def tiles(n, carry):
        wait_tile(n + HALF, 0)
        wait_tile(n + HALF, 1)

        def high_step(i, c):
            tile_step(n + HALF, 0, i)
            return c

        lax.fori_loop(0, 8, high_step, 0)
        wait_tile(n, 1)
        wait_tile(n, 2)

        def low_step(i, c):
            tile_step(n, 4, i)
            return c

        lax.fori_loop(0, 8, low_step, 0)
        return carry

    lax.fori_loop(0, HALF, tiles, 0)

    pl.semaphore_wait(rows_sem, 2)
    lane32 = lax.broadcasted_iota(jnp.int32, (32, LANES), 1)
    lane16 = lax.broadcasted_iota(jnp.int32, (16, LANES), 1)

    def reduce_copies(a, holder):
        k = (row * ROW + a - 4 + 32) % 32
        slot = holder * ROW + own
        return [
            (stage.at[a], reduced.at[slot, pl.ds(0, 2)], 0, k),
            (stage.at[a, pl.ds(0, 1)], reduced.at[slot, pl.ds(2, 1)], 1, (k + 1) % 32),
            (stage.at[a, pl.ds(1, 1)], reduced.at[slot, pl.ds(3, 1)], 2, (k + 4) % 32),
        ]

    for a in range(SLOTS):
        top = acc[a, pl.ds(0, 32), :]
        bottom = acc[a, pl.ds(32, 32), :]
        swapped = jnp.where(
            lane32 % 64 < 32, pltpu.roll(bottom, 96, 1), -pltpu.roll(bottom, 32, 1)
        )
        value = top + swapped
        turned = pltpu.roll(value, 64, 1)
        stage[a, 0] = jnp.where(lane16 < 64, value[:16], turned[16:])
        stage[a, 1] = jnp.where(lane16 < 64, turned[:16], value[16:])
        for src, dst, kind, target in reduce_copies(a, 1 if a < 4 else 0):
            @pl.when(target == me)
            def _():
                pltpu.make_async_copy(src, dst, rrecv_sem.at[kind, 1 if a < 4 else 0]).start()

            @pl.when(target != me)
            def _():
                pltpu.make_async_remote_copy(
                    src_ref=src, dst_ref=dst, send_sem=rsend_sem.at[a, kind],
                    recv_sem=rrecv_sem.at[kind, 1 if a < 4 else 0],
                    device_id={"ka": target}, device_id_type=MESH,
                ).start()

    def wait_reduced(kind, holder):
        first, count = ((0, 2), (2, 1), (3, 1))[kind]
        block = reduced.at[pl.ds(holder * ROW, ROW), pl.ds(first, count)]
        pltpu.make_async_copy(block, block, rrecv_sem.at[kind, holder]).wait()

    def sum_reduced(kind, holder):
        first, count = ((0, 2), (2, 1), (3, 1))[kind]
        value = reduced[holder * ROW, pl.ds(first, count)]
        for j in range(1, ROW):
            value = value + reduced[holder * ROW + j, pl.ds(first, count)]
        return value

    for kind in range(3):
        first, count = ((0, 2), (2, 1), (3, 1))[kind]
        wait_reduced(kind, 0)
        total[pl.ds(first, count)] = sum_reduced(kind, 0)
        source = (own - (0, 1, 4)[kind] + ROW) % ROW

        @pl.when(source >= 4)
        def _():
            wait_reduced(kind, 1)
            total[pl.ds(first, count)] += sum_reduced(kind, 1)

    def slab_copy(dx):
        return pltpu.make_async_remote_copy(
            src_ref=total, dst_ref=gathered.at[gx], send_sem=gsend_sem.at[dx - 1], recv_sem=grecv_sem,
            device_id={"gz": (gx + dx) % 4}, device_id_type=MESH,
        )

    for dx in (1, 2, 3):
        slab_copy(dx).start()
    gathered[gx] = total[...]
    block = gathered.at[pl.ds(0, 3)]
    pltpu.make_async_copy(block, block, grecv_sem).wait()
    summed = gathered[0] + gathered[1] + gathered[2] + gathered[3]
    for index, direction in ((0, 0), (1, 2), (2, 1), (3, 3)):
        value = summed[index]
        real = jnp.concatenate([value[:, 0:32], value[:, 64:96]], axis=0)
        imag = jnp.concatenate([value[:, 32:64], value[:, 96:128]], axis=0)
        if index < 2:
            out_ref[direction, 0] = real
            out_ref[direction, 1] = imag
        else:
            out_ref[direction, 0] = real.T
            out_ref[direction, 1] = -imag.T

    for p in peers:
        pass
    seven = xbuf.at[pl.ds(0, 7)]
    pltpu.make_async_copy(seven, seven, xsend_sem).wait()
    forward_extra().wait_send()

    def drain(t, carry):
        block = buf.at[pl.ds(t * SLOTS, 7)]
        pltpu.make_async_copy(block, block, send_sem.at[t]).wait()
        block = buf.at[pl.ds(t * SLOTS, 4)]
        pltpu.make_async_copy(block, block, fsend_sem.at[t]).wait()
        return carry

    lax.fori_loop(0, TILES, drain, 0)
    for a in range(SLOTS):
        for src, dst, kind, target in reduce_copies(a, 1 if a < 4 else 0):
            @pl.when(target != me)
            def _():
                pltpu.make_async_copy(src, src, rsend_sem.at[a, kind]).wait()
    for dx in (1, 2, 3):
        slab_copy(dx).wait_send()


def per_device(fields, bvectors, gshift):
    local = jnp.transpose(fields[0], (0, 2, 1, 3))
    dma = pltpu.SemaphoreType.DMA
    f32 = jnp.float32
    result = pl.pallas_call(
        kernel,
        out_shape=jax.ShapeDtypeStruct((4, 2, 32, 32), f32),
        in_specs=[
            pl.BlockSpec(memory_space=pltpu.SMEM),
            pl.BlockSpec(memory_space=pltpu.SMEM),
            pl.BlockSpec(memory_space=pltpu.HBM),
        ],
        out_specs=pl.BlockSpec(memory_space=pltpu.VMEM),
        scratch_shapes=[
            pltpu.VMEM((TILES * SLOTS, 2, 3, 32, LANES), f32),
            pltpu.VMEM((SLOTS, 2, 32, LANES), f32),
            pltpu.VMEM((TILES + 1, 2, 16, LANES), f32),
            pltpu.VMEM((SLOTS, 64, LANES), f32),
            pltpu.VMEM((SLOTS, 2, 16, LANES), f32),
            pltpu.VMEM((2 * ROW, 4, 16, LANES), f32),
            pltpu.VMEM((4, 16, LANES), f32),
            pltpu.VMEM((4, 4, 16, LANES), f32),
            dma((TILES,)),
            dma((TILES, 3)),
            dma,
            dma((3,)),
            dma((TILES,)),
            dma,
            dma((SLOTS, 3)),
            dma((3, 2)),
            dma((3,)),
            dma,
            pltpu.SemaphoreType.REGULAR,
        ],
        compiler_params=pltpu.CompilerParams(
            collective_id=0, has_side_effects=True, vmem_limit_bytes=40 * 1024 * 1024
        ),
        name="wannier",
    )(bvectors, jnp.transpose(gshift, (2, 1, 0)), local)
    return result[None]


def solution(mesh):
    in_specs = (P("ka", None, None, None, "gz"), P(), P())
    out_specs = P("ka", None, None, None, None)
    return jax.shard_map(
        per_device, mesh=mesh, in_specs=in_specs, out_specs=out_specs, check_vma=False
    )
```

```python
import math

import jax
import jax.numpy as jnp
from jax import lax
from jax.experimental import pallas as pl
from jax.experimental.pallas import tpu as pltpu
from jax.sharding import PartitionSpec as P

GX = 40
GY = 40
NZ = 16
ROW = 8
ROWS = 4
SLOTS = 12
TILES = 6
LANES = 128
MESH = pl.DeviceIdType.MESH
TWO_PI = 2.0 * math.pi


def split(value):
    high = value.astype(jnp.bfloat16)
    low = (value - high.astype(jnp.float32)).astype(jnp.bfloat16)
    return high, low


def contract(left, right):
    return lax.dot_general(
        left, right, (((1,), (1,)), ((), ())), preferred_element_type=jnp.float32
    )


def kernel(
    bvec_hbm, gshift_hbm, field_ref, out_ref,
    bvec_ref, gshift_ref, buf, xbuf, phase, acc, stage, reduced, total, gathered,
    small_sem, send_sem, recv_sem, xsend_sem, xrecv_sem, fsend_sem, xfsend_sem,
    rsend_sem, rrecv_sem, gsend_sem, grecv_sem, rows_sem,
):
    me = lax.axis_index("ka")
    gx = lax.axis_index("gz")
    row = me // ROW
    own = me % ROW
    zpos = own // 2
    core = own % 2
    side = zpos // 2
    row_up = (row + 1) % ROWS
    row_down = (row + ROWS - 1) % ROWS
    pass_row = jnp.where(core == 0, row_down, row_up)
    pass_from = 8 * core
    pass_to = 8 - 8 * core
    first_k = row * ROW - 4 * core

    def at(r, j):
        return {"ka": r * ROW + j}

    small = [
        pltpu.make_async_copy(bvec_hbm, bvec_ref, small_sem.at[0]),
        pltpu.make_async_copy(gshift_hbm, gshift_ref, small_sem.at[1]),
    ]
    for copy in small:
        copy.start()

    sibling = zpos * 2 + 1 - core
    others = [((zpos + dz) % 4) * 2 for dz in (2, 1, 3)]
    peers = [z + c for z in others for c in range(2)] + [sibling]

    barrier = pltpu.get_barrier_semaphore()
    for p in peers:
        pl.semaphore_signal(barrier, inc=1, device_id=at(row, p), device_id_type=MESH)
    for r in (row_up, row_down):
        pl.semaphore_signal(barrier, inc=1, device_id=at(r, own), device_id_type=MESH)
    for dx in (1, 2, 3):
        pl.semaphore_signal(barrier, inc=1, device_id={"gz": (gx + dx) % 4}, device_id_type=MESH)
    pl.semaphore_wait(barrier, 12)

    def extra_source(p):
        comp = jnp.minimum(p // 2, 2)
        start = pl.multiple_of((ROW * TILES + p % 2) * LANES, LANES)
        return field_ref.at[:, comp, :, pl.ds(start, LANES)]

    def tile_source(p, t):
        start = pl.multiple_of((p * TILES + t) * LANES, LANES)
        return field_ref.at[:, :, :, pl.ds(start, LANES)]

    def send_extra(p, c):
        return pltpu.make_async_remote_copy(
            src_ref=extra_source(p), dst_ref=xbuf.at[own + 4 * c],
            send_sem=xsend_sem, recv_sem=xrecv_sem.at[side + c],
            device_id=at(row, p), device_id_type=MESH,
        )

    def send_tile(p, c, t):
        return pltpu.make_async_remote_copy(
            src_ref=tile_source(p, t), dst_ref=buf.at[t * SLOTS + own + 4 * c],
            send_sem=send_sem.at[t], recv_sem=recv_sem.at[t, side + c],
            device_id=at(row, p), device_id_type=MESH,
        )

    for z in others:
        for c in range(2):
            send_extra(z + c, c).start()
    send_extra(sibling, 1 - core).start()
    pltpu.make_async_copy(
        extra_source(own), xbuf.at[own + 4 * core], xrecv_sem.at[side + core]
    ).start()

    def send_first(t, carry):
        for z in others:
            send_tile(z + side, side, t).start()
        send_tile(sibling, 1 - core, t).start()
        pltpu.make_async_copy(
            tile_source(own, t), buf.at[t * SLOTS + own + 4 * core], recv_sem.at[t, side + core]
        ).start()
        return carry

    def send_second(t, carry):
        for z in others:
            send_tile(z + 1 - side, 1 - side, t).start()
        return carry

    lax.fori_loop(0, TILES, send_first, 0)
    lax.fori_loop(0, TILES, send_second, 0)

    for r in (row_up, row_down):
        pl.semaphore_signal(rows_sem, inc=1, device_id=at(r, own), device_id_type=MESH)

    for copy in small:
        copy.wait()

    row_id = lax.broadcasted_iota(jnp.int32, (16, LANES), 0)
    lane = lax.broadcasted_iota(jnp.int32, (16, LANES), 1).astype(jnp.float32)
    q = []
    for a in range(3):
        values = jnp.zeros((16, LANES), jnp.float32)
        for d in range(2):
            for i in range(8):
                k = (first_k + i + 32) % 32
                value = bvec_ref[d, a] + gshift_ref[a, d, k].astype(jnp.float32)
                values = jnp.where(row_id == d * 8 + i, value, values)
        q.append(values)

    def write_phase(index, start, keep):
        cell = lane + start.astype(jnp.float32)
        line = jnp.floor((cell + 0.5) * (1.0 / GX))
        plane = jnp.floor((cell + 0.5) * (1.0 / (GX * GY)))
        xc = cell - GX * line
        yc = line - GY * plane
        zc = plane + (gx * 4).astype(jnp.float32)
        theta = -TWO_PI * (q[0] * xc / GX + q[1] * yc / GY + q[2] * zc / NZ)
        phase[index, 0] = jnp.cos(theta) * keep
        phase[index, 1] = jnp.sin(theta) * keep

    def tile_phase(t, carry):
        write_phase(t, (own * TILES + t) * LANES, 1.0)
        return carry

    lax.fori_loop(0, TILES, tile_phase, 0)
    write_phase(TILES, (ROW * TILES + own % 2) * LANES, (own < 6).astype(jnp.float32))
    acc[...] = jnp.zeros_like(acc)

    def wait_tile(t, group):
        block = buf.at[pl.ds(t * SLOTS + 4 * group, 4)]
        pltpu.make_async_copy(block, block, recv_sem.at[t, group]).wait()

    def wait_extra(group):
        block = xbuf.at[pl.ds(4 * group, 4)]
        pltpu.make_async_copy(block, block, xrecv_sem.at[group]).wait()

    pass_extra = pltpu.make_async_remote_copy(
        src_ref=xbuf.at[pl.ds(pass_from, 4)], dst_ref=xbuf.at[pl.ds(pass_to, 4)],
        send_sem=xfsend_sem, recv_sem=xrecv_sem.at[2 - 2 * core],
        device_id=at(pass_row, own), device_id_type=MESH,
    )

    def pass_tile(t, carry):
        wait_tile(t, 2 * core)
        pltpu.make_async_remote_copy(
            src_ref=buf.at[pl.ds(t * SLOTS + pass_from, 4)],
            dst_ref=buf.at[pl.ds(t * SLOTS + pass_to, 4)],
            send_sem=fsend_sem.at[t], recv_sem=recv_sem.at[t, 2 - 2 * core],
            device_id=at(pass_row, own), device_id_type=MESH,
        ).start()
        return carry

    wait_extra(2 * core)
    pass_extra.start()
    lax.fori_loop(0, TILES, pass_tile, 0)

    def pair_products(left, rights):
        left_high, left_low = split(left)
        right_high, right_low = split(jnp.concatenate(rights, axis=0))
        return (
            contract(left_high, right_high)
            + contract(left_high, right_low)
            + contract(left_low, right_high)
        )

    def rotate(real, imag, index, d, i, comps):
        c = phase[index, 0, pl.ds(d * 8 + i, 1), :]
        s = phase[index, 1, pl.ds(d * 8 + i, 1), :]
        c = jnp.concatenate([jnp.broadcast_to(c, (32, LANES))] * comps, axis=1)
        s = jnp.concatenate([jnp.broadcast_to(s, (32, LANES))] * comps, axis=1)
        return [c * real - s * imag, s * real + c * imag]

    def extra_step(i):
        left = xbuf[i].reshape(64, LANES)
        rights = []
        for d, offset in enumerate((1, 4)):
            rights += rotate(xbuf[i + offset, 0], xbuf[i + offset, 1], TILES, d, i, 1)
        acc[i] += pair_products(left, rights)

    def wide(slot, part):
        return jnp.concatenate([buf[slot, part, comp] for comp in range(3)], axis=1)

    def tile_step(t, i):
        base = t * SLOTS + i
        left = jnp.concatenate([wide(base, 0), wide(base, 1)], axis=0)
        rights = []
        for d, offset in enumerate((1, 4)):
            rights += rotate(wide(base + offset, 0), wide(base + offset, 1), t, d, i, 3)
        acc[i] += pair_products(left, rights)

    lane32 = lax.broadcasted_iota(jnp.int32, (32, LANES), 1)
    lane16 = lax.broadcasted_iota(jnp.int32, (16, LANES), 1)
    holder = core * 4 + zpos
    kinds = ((0, 2), (2, 1), (3, 1))

    def reduce_copies(i):
        k = first_k + i + 32
        return [
            (stage.at[i], reduced.at[holder, pl.ds(0, 2)], 0, k % 32),
            (stage.at[i, pl.ds(0, 1)], reduced.at[holder, pl.ds(2, 1)], 1, (k + 1) % 32),
            (stage.at[i, pl.ds(1, 1)], reduced.at[holder, pl.ds(3, 1)], 2, (k + 4) % 32),
        ]

    def send_matrices(i):
        top = acc[i, pl.ds(0, 32), :]
        bottom = acc[i, pl.ds(32, 32), :]
        swapped = jnp.where(
            lane32 % 64 < 32, pltpu.roll(bottom, 96, 1), -pltpu.roll(bottom, 32, 1)
        )
        value = top + swapped
        turned = pltpu.roll(value, 64, 1)
        stage[i, 0] = jnp.where(lane16 < 64, value[:16], turned[16:])
        stage[i, 1] = jnp.where(lane16 < 64, turned[:16], value[16:])
        for src, dst, kind, target in reduce_copies(i):
            @pl.when(target == me)
            def _():
                pltpu.make_async_copy(src, dst, rrecv_sem.at[kind]).start()

            @pl.when(target != me)
            def _():
                pltpu.make_async_remote_copy(
                    src_ref=src, dst_ref=dst, send_sem=rsend_sem.at[i, kind],
                    recv_sem=rrecv_sem.at[kind],
                    device_id={"ka": target}, device_id_type=MESH,
                ).start()

    def loop(step):
        def body(m, carry):
            step(2 * m)
            step(2 * m + 1)
            return carry

        lax.fori_loop(0, 4, body, 0)

    wait_extra(1)
    wait_extra(2 - 2 * core)
    loop(extra_step)

    def tiles(t, carry):
        wait_tile(t, 2 - 2 * core)
        wait_tile(t, 1)
        loop(lambda i: tile_step(t, i))
        return carry

    lax.fori_loop(0, TILES - 1, tiles, 0)
    pl.semaphore_wait(rows_sem, 2)
    wait_tile(TILES - 1, 2 - 2 * core)
    wait_tile(TILES - 1, 1)

    def last(m, carry):
        tile_step(TILES - 1, 2 * m)
        tile_step(TILES - 1, 2 * m + 1)
        send_matrices(2 * m)
        send_matrices(2 * m + 1)
        return carry

    lax.fori_loop(0, 4, last, 0)

    for kind, (first, count) in enumerate(kinds):
        block = reduced.at[:, pl.ds(first, count)]
        pltpu.make_async_copy(block, block, rrecv_sem.at[kind]).wait()
        value = reduced[0, pl.ds(first, count)]
        for j in range(1, ROW):
            value = value + reduced[j, pl.ds(first, count)]
        total[pl.ds(first, count)] = value

    def slab_copy(dx):
        return pltpu.make_async_remote_copy(
            src_ref=total, dst_ref=gathered.at[gx], send_sem=gsend_sem.at[dx - 1], recv_sem=grecv_sem,
            device_id={"gz": (gx + dx) % 4}, device_id_type=MESH,
        )

    for dx in (2, 1, 3):
        slab_copy(dx).start()
    gathered[gx] = total[...]

    seven = xbuf.at[pl.ds(0, 7)]
    pltpu.make_async_copy(seven, seven, xsend_sem).wait()
    pass_extra.wait_send()

    def drain(t, carry):
        block = buf.at[pl.ds(t * SLOTS, 7)]
        pltpu.make_async_copy(block, block, send_sem.at[t]).wait()
        block = buf.at[pl.ds(t * SLOTS, 4)]
        pltpu.make_async_copy(block, block, fsend_sem.at[t]).wait()
        return carry

    lax.fori_loop(0, TILES, drain, 0)

    def drain_matrices(i, carry):
        for src, dst, kind, target in reduce_copies(i):
            @pl.when(target != me)
            def _():
                pltpu.make_async_copy(src, src, rsend_sem.at[i, kind]).wait()
        return carry

    lax.fori_loop(0, 8, drain_matrices, 0)

    block = gathered.at[pl.ds(0, 3)]
    pltpu.make_async_copy(block, block, grecv_sem).wait()
    summed = gathered[0] + gathered[1] + gathered[2] + gathered[3]
    for index, direction in ((0, 0), (1, 2), (2, 1), (3, 3)):
        value = summed[index]
        real = jnp.concatenate([value[:, 0:32], value[:, 64:96]], axis=0)
        imag = jnp.concatenate([value[:, 32:64], value[:, 96:128]], axis=0)
        if index < 2:
            out_ref[direction, 0] = real
            out_ref[direction, 1] = imag
        else:
            out_ref[direction, 0] = real.T
            out_ref[direction, 1] = -imag.T
    for dx in (1, 2, 3):
        slab_copy(dx).wait_send()


def per_device(fields, bvectors, gshift):
    local = jnp.transpose(fields[0], (0, 2, 1, 3))
    dma = pltpu.SemaphoreType.DMA
    f32 = jnp.float32
    result = pl.pallas_call(
        kernel,
        out_shape=jax.ShapeDtypeStruct((4, 2, 32, 32), f32),
        in_specs=[
            pl.BlockSpec(memory_space=pltpu.HBM),
            pl.BlockSpec(memory_space=pltpu.HBM),
            pl.BlockSpec(memory_space=pltpu.HBM),
        ],
        out_specs=pl.BlockSpec(memory_space=pltpu.VMEM),
        scratch_shapes=[
            pltpu.SMEM((2, 3), f32),
            pltpu.SMEM((3, 2, 32), jnp.int32),
            pltpu.VMEM((TILES * SLOTS, 2, 3, 32, LANES), f32),
            pltpu.VMEM((SLOTS, 2, 32, LANES), f32),
            pltpu.VMEM((TILES + 1, 2, 16, LANES), f32),
            pltpu.VMEM((ROW, 64, LANES), f32),
            pltpu.VMEM((ROW, 2, 16, LANES), f32),
            pltpu.VMEM((ROW, 4, 16, LANES), f32),
            pltpu.VMEM((4, 16, LANES), f32),
            pltpu.VMEM((4, 4, 16, LANES), f32),
            dma((2,)),
            dma((TILES,)),
            dma((TILES, 3)),
            dma,
            dma((3,)),
            dma((TILES,)),
            dma,
            dma((ROW, 3)),
            dma((3,)),
            dma((3,)),
            dma,
            pltpu.SemaphoreType.REGULAR,
        ],
        compiler_params=pltpu.CompilerParams(
            collective_id=0, has_side_effects=True, vmem_limit_bytes=60 * 1024 * 1024
        ),
        name="wannier",
    )(bvectors, jnp.transpose(gshift, (2, 1, 0)), local)
    return result[None]


def solution(mesh):
    in_specs = (P("ka", None, None, None, "gz"), P(), P())
    out_specs = P("ka", None, None, None, None)
    return jax.shard_map(
        per_device, mesh=mesh, in_specs=in_specs, out_specs=out_specs, check_vma=False
    )
```

```python
import math

import jax
import jax.numpy as jnp
from jax import lax
from jax.experimental import pallas as pl
from jax.experimental.pallas import tpu as pltpu
from jax.sharding import PartitionSpec as P

GX = 40
GY = 40
NZ = 16
ROW = 8
ROWS = 4
SLOTS = 12
TILES = 6
LANES = 128
UNROLL = 8
MESH = pl.DeviceIdType.MESH
TWO_PI = 2.0 * math.pi


def split(value):
    high = value.astype(jnp.bfloat16)
    low = (value - high.astype(jnp.float32)).astype(jnp.bfloat16)
    return high, low


def contract(left, right):
    return lax.dot_general(
        left, right, (((1,), (1,)), ((), ())), preferred_element_type=jnp.float32
    )


def kernel(
    bvec_hbm, gshift_hbm, field_ref, out_ref,
    bvec_ref, gshift_ref, buf, xbuf, phase, acc, stage, reduced, total, gathered,
    small_sem, send_sem, recv_sem, xsend_sem, xrecv_sem, fsend_sem, xfsend_sem,
    rsend_sem, rrecv_sem, gsend_sem, grecv_sem, rows_sem,
):
    me = lax.axis_index("ka")
    gx = lax.axis_index("gz")
    row = me // ROW
    own = me % ROW
    zpos = own // 2
    core = own % 2
    side = zpos // 2
    row_up = (row + 1) % ROWS
    row_down = (row + ROWS - 1) % ROWS
    pass_row = jnp.where(core == 0, row_down, row_up)
    pass_from = 8 * core
    pass_to = 8 - 8 * core
    first_k = row * ROW - 4 * core

    def at(r, j):
        return {"ka": r * ROW + j}

    small = [
        pltpu.make_async_copy(bvec_hbm, bvec_ref, small_sem.at[0]),
        pltpu.make_async_copy(gshift_hbm, gshift_ref, small_sem.at[1]),
    ]
    for copy in small:
        copy.start()

    sibling = zpos * 2 + 1 - core
    others = [((zpos + dz) % 4) * 2 for dz in (2, 1, 3)]
    peers = [z + c for z in others for c in range(2)] + [sibling]

    barrier = pltpu.get_barrier_semaphore()
    for p in peers:
        pl.semaphore_signal(barrier, inc=1, device_id=at(row, p), device_id_type=MESH)
    for r in (row_up, row_down):
        pl.semaphore_signal(barrier, inc=1, device_id=at(r, own), device_id_type=MESH)
    for dx in (1, 2, 3):
        pl.semaphore_signal(barrier, inc=1, device_id={"gz": (gx + dx) % 4}, device_id_type=MESH)
    pl.semaphore_wait(barrier, 12)

    def extra_source(p):
        comp = jnp.minimum(p // 2, 2)
        start = pl.multiple_of((ROW * TILES + p % 2) * LANES, LANES)
        return field_ref.at[:, comp, :, pl.ds(start, LANES)]

    def tile_source(p, t):
        start = pl.multiple_of((p * TILES + t) * LANES, LANES)
        return field_ref.at[:, :, :, pl.ds(start, LANES)]

    def send_extra(p, c):
        return pltpu.make_async_remote_copy(
            src_ref=extra_source(p), dst_ref=xbuf.at[own + 4 * c],
            send_sem=xsend_sem, recv_sem=xrecv_sem.at[side + c],
            device_id=at(row, p), device_id_type=MESH,
        )

    def send_tile(p, c, t):
        return pltpu.make_async_remote_copy(
            src_ref=tile_source(p, t), dst_ref=buf.at[t * SLOTS + own + 4 * c],
            send_sem=send_sem.at[t], recv_sem=recv_sem.at[t, side + c],
            device_id=at(row, p), device_id_type=MESH,
        )

    for z in others:
        send_extra(z + side, side).start()
    send_extra(sibling, 1 - core).start()
    pltpu.make_async_copy(
        extra_source(own), xbuf.at[own + 4 * core], xrecv_sem.at[side + core]
    ).start()

    def send_first(t, carry):
        for z in others:
            send_tile(z + side, side, t).start()
        send_tile(sibling, 1 - core, t).start()
        pltpu.make_async_copy(
            tile_source(own, t), buf.at[t * SLOTS + own + 4 * core], recv_sem.at[t, side + core]
        ).start()
        return carry

    def send_second(t, carry):
        for z in others:
            send_tile(z + 1 - side, 1 - side, t).start()
        return carry

    lax.fori_loop(0, TILES, send_first, 0)
    lax.fori_loop(0, TILES, send_second, 0)
    for z in others:
        send_extra(z + 1 - side, 1 - side).start()

    for r in (row_up, row_down):
        pl.semaphore_signal(rows_sem, inc=1, device_id=at(r, own), device_id_type=MESH)

    for copy in small:
        copy.wait()

    row_id = lax.broadcasted_iota(jnp.int32, (16, LANES), 0)
    lane = lax.broadcasted_iota(jnp.int32, (16, LANES), 1).astype(jnp.float32)
    q = []
    for a in range(3):
        values = jnp.zeros((16, LANES), jnp.float32)
        for d in range(2):
            for i in range(8):
                k = (first_k + i + 32) % 32
                value = bvec_ref[d, a] + gshift_ref[a, d, k].astype(jnp.float32)
                values = jnp.where(row_id == d * 8 + i, value, values)
        q.append(values)

    def write_phase(index, start, keep):
        cell = lane + start.astype(jnp.float32)
        line = jnp.floor((cell + 0.5) * (1.0 / GX))
        plane = jnp.floor((cell + 0.5) * (1.0 / (GX * GY)))
        xc = cell - GX * line
        yc = line - GY * plane
        zc = plane + (gx * 4).astype(jnp.float32)
        theta = -TWO_PI * (q[0] * xc / GX + q[1] * yc / GY + q[2] * zc / NZ)
        phase[index, 0] = jnp.cos(theta) * keep
        phase[index, 1] = jnp.sin(theta) * keep

    def tile_phase(t, carry):
        write_phase(t, (own * TILES + t) * LANES, 1.0)
        return carry

    lax.fori_loop(0, TILES, tile_phase, 0)
    write_phase(TILES, (ROW * TILES + own % 2) * LANES, (own < 6).astype(jnp.float32))
    acc[...] = jnp.zeros_like(acc)

    def wait_tile(t, group):
        block = buf.at[pl.ds(t * SLOTS + 4 * group, 4)]
        pltpu.make_async_copy(block, block, recv_sem.at[t, group]).wait()

    def wait_extra(group):
        block = xbuf.at[pl.ds(4 * group, 4)]
        pltpu.make_async_copy(block, block, xrecv_sem.at[group]).wait()

    pass_extra = pltpu.make_async_remote_copy(
        src_ref=xbuf.at[pl.ds(pass_from, 4)], dst_ref=xbuf.at[pl.ds(pass_to, 4)],
        send_sem=xfsend_sem, recv_sem=xrecv_sem.at[2 - 2 * core],
        device_id=at(pass_row, own), device_id_type=MESH,
    )

    def pass_tile(t, carry):
        wait_tile(t, 2 * core)
        pltpu.make_async_remote_copy(
            src_ref=buf.at[pl.ds(t * SLOTS + pass_from, 4)],
            dst_ref=buf.at[pl.ds(t * SLOTS + pass_to, 4)],
            send_sem=fsend_sem.at[t], recv_sem=recv_sem.at[t, 2 - 2 * core],
            device_id=at(pass_row, own), device_id_type=MESH,
        ).start()
        return carry

    wait_extra(2 * core)
    pass_extra.start()
    lax.fori_loop(0, TILES, pass_tile, 0)

    def pair_products(left, rights):
        left_high, left_low = split(left)
        right_high, right_low = split(jnp.concatenate(rights, axis=0))
        return (
            contract(left_high, right_high)
            + contract(left_high, right_low)
            + contract(left_low, right_high)
        )

    def rotate(real, imag, index, d, i, comps):
        c = phase[index, 0, pl.ds(d * 8 + i, 1), :]
        s = phase[index, 1, pl.ds(d * 8 + i, 1), :]
        c = jnp.concatenate([jnp.broadcast_to(c, (32, LANES))] * comps, axis=1)
        s = jnp.concatenate([jnp.broadcast_to(s, (32, LANES))] * comps, axis=1)
        return [c * real - s * imag, s * real + c * imag]

    def extra_step(i):
        left = xbuf[i].reshape(64, LANES)
        rights = []
        for d, offset in enumerate((1, 4)):
            rights += rotate(xbuf[i + offset, 0], xbuf[i + offset, 1], TILES, d, i, 1)
        acc[i] += pair_products(left, rights)

    def wide(slot, part):
        return jnp.concatenate([buf[slot, part, comp] for comp in range(3)], axis=1)

    def tile_step(t, i):
        base = t * SLOTS + i
        left = jnp.concatenate([wide(base, 0), wide(base, 1)], axis=0)
        rights = []
        for d, offset in enumerate((1, 4)):
            rights += rotate(wide(base + offset, 0), wide(base + offset, 1), t, d, i, 3)
        acc[i] += pair_products(left, rights)

    lane32 = lax.broadcasted_iota(jnp.int32, (32, LANES), 1)
    lane16 = lax.broadcasted_iota(jnp.int32, (16, LANES), 1)
    holder = core * 4 + zpos
    spans = [(0, 2)] + [(0, 3)] * 3 + [(0, 4)] * 4 + [(2, 2)] + [(3, 1)] * 3

    def target_copy(i):
        part = pl.ds(*spans[i])
        target = (first_k + i + 32) % 32
        return target, pltpu.make_async_remote_copy(
            src_ref=stage.at[i, part], dst_ref=reduced.at[holder, part],
            send_sem=rsend_sem.at[i], recv_sem=rrecv_sem,
            device_id={"ka": target}, device_id_type=MESH,
        )

    def send_target(i):
        part = pl.ds(*spans[i])
        target, copy = target_copy(i)

        @pl.when(target == me)
        def _():
            pltpu.make_async_copy(stage.at[i, part], reduced.at[holder, part], rrecv_sem).start()

        @pl.when(target != me)
        def _():
            copy.start()

    def finish_matrices(i):
        top = acc[i, pl.ds(0, 32), :]
        bottom = acc[i, pl.ds(32, 32), :]
        swapped = jnp.where(
            lane32 % 64 < 32, pltpu.roll(bottom, 96, 1), -pltpu.roll(bottom, 32, 1)
        )
        value = top + swapped
        turned = pltpu.roll(value, 64, 1)
        along_x = jnp.where(lane16 < 64, value[:16], turned[16:])
        along_y = jnp.where(lane16 < 64, turned[:16], value[16:])
        stage[i, 0] = along_x
        stage[i, 1] = along_y
        stage[i + 1, 2] = along_x
        stage[i + 4, 3] = along_y

    def tiles(t, carry):
        wait_tile(t, 2 - 2 * core)
        wait_tile(t, 1)

        def body(m, inner):
            for u in range(UNROLL):
                tile_step(t, UNROLL * m + u)
            return inner

        lax.fori_loop(0, ROW // UNROLL, body, 0)
        return carry

    lax.fori_loop(0, TILES, tiles, 0)
    pl.semaphore_wait(rows_sem, 2)
    wait_extra(2 - 2 * core)
    wait_extra(1)
    for i in range(ROW):
        extra_step(i)
        finish_matrices(i)
    for i in range(SLOTS):
        send_target(i)

    def slab_copy(dx):
        return pltpu.make_async_remote_copy(
            src_ref=total, dst_ref=gathered.at[gx],
            send_sem=gsend_sem.at[dx - 1], recv_sem=grecv_sem,
            device_id={"gz": (gx + dx) % 4}, device_id_type=MESH,
        )

    pltpu.make_async_copy(reduced, reduced, rrecv_sem).wait()
    value = reduced[0]
    for j in range(1, ROW):
        value = value + reduced[j]
    total[...] = value
    for dx in (2, 1, 3):
        slab_copy(dx).start()
    gathered[gx] = value

    seven = xbuf.at[pl.ds(0, 7)]
    pltpu.make_async_copy(seven, seven, xsend_sem).wait()
    pass_extra.wait_send()

    def drain(t, carry):
        block = buf.at[pl.ds(t * SLOTS, 7)]
        pltpu.make_async_copy(block, block, send_sem.at[t]).wait()
        block = buf.at[pl.ds(t * SLOTS, 4)]
        pltpu.make_async_copy(block, block, fsend_sem.at[t]).wait()
        return carry

    lax.fori_loop(0, TILES, drain, 0)

    for i in range(SLOTS):
        target, copy = target_copy(i)

        @pl.when(target != me)
        def _():
            copy.wait_send()

    block = gathered.at[pl.ds(0, 3)]
    pltpu.make_async_copy(block, block, grecv_sem).wait()
    summed = gathered[0] + gathered[1] + gathered[2] + gathered[3]
    for index, direction in ((0, 0), (1, 2), (2, 1), (3, 3)):
        value = summed[index]
        real = jnp.concatenate([value[:, 0:32], value[:, 64:96]], axis=0)
        imag = jnp.concatenate([value[:, 32:64], value[:, 96:128]], axis=0)
        if index < 2:
            out_ref[direction, 0] = real
            out_ref[direction, 1] = imag
        else:
            out_ref[direction, 0] = real.T
            out_ref[direction, 1] = -imag.T
    for dx in (1, 2, 3):
        slab_copy(dx).wait_send()


def per_device(fields, bvectors, gshift):
    local, vectors, shifts = (
        pltpu.with_memory_space_constraint(value, pltpu.HBM)
        for value in (
            jnp.transpose(fields[0], (0, 2, 1, 3)), bvectors, jnp.transpose(gshift, (2, 1, 0))
        )
    )
    dma = pltpu.SemaphoreType.DMA
    f32 = jnp.float32
    result = pl.pallas_call(
        kernel,
        out_shape=jax.ShapeDtypeStruct((4, 2, 32, 32), f32),
        in_specs=[
            pl.BlockSpec(memory_space=pltpu.HBM),
            pl.BlockSpec(memory_space=pltpu.HBM),
            pl.BlockSpec(memory_space=pltpu.HBM),
        ],
        out_specs=pl.BlockSpec(memory_space=pltpu.VMEM),
        scratch_shapes=[
            pltpu.SMEM((2, 3), f32),
            pltpu.SMEM((3, 2, 32), jnp.int32),
            pltpu.VMEM((TILES * SLOTS, 2, 3, 32, LANES), f32),
            pltpu.VMEM((SLOTS, 2, 32, LANES), f32),
            pltpu.VMEM((TILES + 1, 2, 16, LANES), f32),
            pltpu.VMEM((ROW, 64, LANES), f32),
            pltpu.VMEM((SLOTS, 4, 16, LANES), f32),
            pltpu.VMEM((ROW, 4, 16, LANES), f32),
            pltpu.VMEM((4, 16, LANES), f32),
            pltpu.VMEM((4, 4, 16, LANES), f32),
            dma((2,)),
            dma((TILES,)),
            dma((TILES, 3)),
            dma,
            dma((3,)),
            dma((TILES,)),
            dma,
            dma((SLOTS,)),
            dma,
            dma((3,)),
            dma,
            pltpu.SemaphoreType.REGULAR,
        ],
        compiler_params=pltpu.CompilerParams(
            collective_id=0, has_side_effects=True, vmem_limit_bytes=40000 * 1024
        ),
        name="wannier",
    )(vectors, shifts, local)
    return result[None]


def solution(mesh):
    in_specs = (P("ka", None, None, None, "gz"), P(), P())
    out_specs = P("ka", None, None, None, None)
    return jax.shard_map(
        per_device, mesh=mesh, in_specs=in_specs, out_specs=out_specs, check_vma=False
    )
```

```python
import math

import jax
import jax.numpy as jnp
from jax import lax
from jax.experimental import pallas as pl
from jax.experimental.pallas import tpu as pltpu
from jax.sharding import PartitionSpec as P

GX = 40
GY = 40
NZ = 16
ROW = 8
ROWS = 4
SLOTS = 12
TILES = 6
LANES = 128
EARLY = ((0, 2), (2, 2), (4, 2))
LATE = ((0, 2), (2, 2), (4, 1), (5, 1))
MESH = pl.DeviceIdType.MESH
TWO_PI = 2.0 * math.pi


def split(value):
    high = value.astype(jnp.bfloat16)
    low = (value - high.astype(jnp.float32)).astype(jnp.bfloat16)
    return high, low


def contract(left, right):
    return lax.dot_general(
        left, right, (((1,), (1,)), ((), ())), preferred_element_type=jnp.float32
    )


def kernel(
    bvec_hbm, gshift_hbm, field_ref, out_ref,
    bvec_ref, gshift_ref, buf, xbuf, phase, acc, stage, reduced, total, gathered,
    small_sem, send_sem, early_sem, late_sem, passed_sem, xsend_sem, xrecv_sem, fsend_sem, xfsend_sem,
    rsend_sem, rrecv_sem, gsend_sem, grecv_sem, rows_sem, across_sem,
):
    me = lax.axis_index("ka")
    gx = lax.axis_index("gz")
    row = me // ROW
    own = me % ROW
    zpos = own // 2
    core = own % 2
    side = zpos // 2
    row_up = (row + 1) % ROWS
    row_down = (row + ROWS - 1) % ROWS
    pass_row = jnp.where(core == 0, row_down, row_up)
    pass_from = 8 * core
    pass_to = 8 - 8 * core
    first_k = row * ROW - 4 * core

    def at(r, j):
        return {"ka": r * ROW + j}

    sibling = zpos * 2 + 1 - core
    others = [((zpos + dz) % 4) * 2 for dz in (1, 3, 2)]
    barrier = pltpu.get_barrier_semaphore()
    near = [at(row, z + c) for z in others[:2] for c in range(2)] + [at(row, sibling)]
    near += [at(row_up, own), at(row_down, own)]
    near += [{"gz": (gx + 1) % 4}, {"gz": (gx + 3) % 4}]
    for device in near:
        pl.semaphore_signal(barrier, inc=1, device_id=device, device_id_type=MESH)
    small = [
        pltpu.make_async_copy(bvec_hbm, bvec_ref, small_sem.at[0]),
        pltpu.make_async_copy(gshift_hbm, gshift_ref, small_sem.at[1]),
    ]
    for copy in small:
        copy.start()

    pl.semaphore_wait(barrier, len(near))
    pl.semaphore_signal(across_sem.at[0], inc=1, device_id=at(row, others[1] + core), device_id_type=MESH)
    pl.semaphore_signal(across_sem.at[1], inc=1, device_id={"gz": (gx + 3) % 4}, device_id_type=MESH)

    def extra_source(p):
        comp = jnp.minimum(p // 2, 2)
        start = pl.multiple_of((ROW * TILES + p % 2) * LANES, LANES)
        return field_ref.at[:, comp, :, pl.ds(start, LANES)]

    def lanes_of(block):
        return pl.ds(block[0] * LANES, block[1] * LANES)

    def block_source(p, block):
        start = pl.multiple_of((p * TILES + block[0]) * LANES, LANES)
        return field_ref.at[:, :, :, pl.ds(start, block[1] * LANES)]

    def block_target(slot, block):
        return buf.at[slot, :, :, :, lanes_of(block)]

    def send_extra(z, c):
        pltpu.make_async_remote_copy(
            src_ref=extra_source(z + c), dst_ref=xbuf.at[own + 4 * c],
            send_sem=xsend_sem, recv_sem=xrecv_sem.at[side + c],
            device_id=at(row, z + c), device_id_type=MESH,
        ).start()

    def keep_extra(c):
        pltpu.make_async_copy(
            extra_source(own), xbuf.at[own + 4 * c], xrecv_sem.at[side + c]
        ).start()

    def send_blocks(z, c, blocks, sems):
        for n, block in blocks:
            pltpu.make_async_remote_copy(
                src_ref=block_source(z + c, block), dst_ref=block_target(own + 4 * c, block),
                send_sem=send_sem, recv_sem=sems.at[n],
                device_id=at(row, z + c), device_id_type=MESH,
            ).start()

    def keep_blocks(c, blocks, sems):
        for n, block in blocks:
            pltpu.make_async_copy(
                block_source(own, block), block_target(own + 4 * c, block), sems.at[n]
            ).start()

    early = list(enumerate(EARLY))
    late = list(enumerate(LATE))
    for z in others[:2]:
        send_extra(z, side)
    for z in others[:2]:
        send_blocks(z, side, early[:1], early_sem)
    pl.semaphore_wait(across_sem.at[0], 1)
    send_extra(others[2], side)
    send_blocks(others[2], side, early[:1], early_sem)
    for pair in early[1:]:
        for z in others:
            send_blocks(z, side, [pair], early_sem)
    here = zpos * 2

    @pl.when(core == side)
    def _():
        keep_extra(side)
        keep_blocks(side, early, early_sem)
        send_extra(here, 1 - side)
        send_blocks(here, 1 - side, late, late_sem)

    @pl.when(core != side)
    def _():
        send_extra(here, side)
        send_blocks(here, side, early, early_sem)
        keep_extra(1 - side)
        keep_blocks(1 - side, late, late_sem)

    for pair in late:
        for z in others:
            send_blocks(z, 1 - side, [pair], late_sem)
    for z in others:
        send_extra(z, 1 - side)

    for r in (row_up, row_down):
        pl.semaphore_signal(rows_sem, inc=1, device_id=at(r, own), device_id_type=MESH)

    for copy in small:
        copy.wait()

    row_id = lax.broadcasted_iota(jnp.int32, (16, LANES), 0)
    lane = lax.broadcasted_iota(jnp.int32, (16, TILES * LANES), 1).astype(jnp.float32)
    q = []
    for a in range(3):
        values = jnp.zeros((16, LANES), jnp.float32)
        for d in range(2):
            for i in range(8):
                k = (first_k + i + 32) % 32
                value = bvec_ref[d, a] + gshift_ref[a, d, k].astype(jnp.float32)
                values = jnp.where(row_id == d * 8 + i, value, values)
        q.append(jnp.concatenate([values] * TILES, axis=1))

    def phases_of(start, width):
        cell = lane[:, :width] + start.astype(jnp.float32)
        line = jnp.floor((cell + 0.5) * (1.0 / GX))
        plane = jnp.floor((cell + 0.5) * (1.0 / (GX * GY)))
        xc = cell - GX * line
        yc = line - GY * plane
        zc = plane + (gx * 4).astype(jnp.float32)
        q0, q1, q2 = (values[:, :width] for values in q)
        theta = -TWO_PI * (q0 * xc / GX + q1 * yc / GY + q2 * zc / NZ)
        return jnp.cos(theta), jnp.sin(theta)

    cosine, sine = phases_of(own * TILES * LANES, TILES * LANES)
    phase[0, :, pl.ds(0, TILES * LANES)] = cosine
    phase[1, :, pl.ds(0, TILES * LANES)] = sine
    cosine, sine = phases_of((ROW * TILES + own % 2) * LANES, LANES)
    keep = (own < 6).astype(jnp.float32)
    phase[0, :, pl.ds(TILES * LANES, LANES)] = cosine * keep
    phase[1, :, pl.ds(TILES * LANES, LANES)] = sine * keep
    acc[...] = jnp.zeros_like(acc)

    def wait_block(group, block, sem):
        target = block_target(pl.ds(4 * group, 4), block)
        pltpu.make_async_copy(target, target, sem).wait()

    def wait_extra(group):
        block = xbuf.at[pl.ds(4 * group, 4)]
        pltpu.make_async_copy(block, block, xrecv_sem.at[group]).wait()

    pass_extra = pltpu.make_async_remote_copy(
        src_ref=xbuf.at[pl.ds(pass_from, 4)], dst_ref=xbuf.at[pl.ds(pass_to, 4)],
        send_sem=xfsend_sem, recv_sem=xrecv_sem.at[2 - 2 * core],
        device_id=at(pass_row, own), device_id_type=MESH,
    )

    def pass_block(n, block):
        return pltpu.make_async_remote_copy(
            src_ref=block_target(pl.ds(pass_from, 4), block),
            dst_ref=block_target(pl.ds(pass_to, 4), block),
            send_sem=fsend_sem.at[n], recv_sem=passed_sem.at[n],
            device_id=at(pass_row, own), device_id_type=MESH,
        )

    wait_extra(2 * core)
    pass_extra.start()
    for n, block in early:
        wait_block(2 * core, block, early_sem.at[n])
        pass_block(n, block).start()

    def pair_products(left, rights):
        left_high, left_low = split(left)
        right_high, right_low = split(jnp.concatenate(rights, axis=0))
        return (
            contract(left_high, right_high)
            + contract(left_high, right_low)
            + contract(left_low, right_high)
        )

    def rotate(real, imag, lanes, d, i, comps):
        c = phase[0, pl.ds(d * 8 + i, 1), lanes]
        s = phase[1, pl.ds(d * 8 + i, 1), lanes]
        width = c.shape[1]
        c = jnp.concatenate([jnp.broadcast_to(c, (32, width))] * comps, axis=1)
        s = jnp.concatenate([jnp.broadcast_to(s, (32, width))] * comps, axis=1)
        return [c * real - s * imag, s * real + c * imag]

    def extra_step(i):
        left = xbuf[i].reshape(64, LANES)
        lanes = pl.ds(TILES * LANES, LANES)
        rights = []
        for d, offset in enumerate((1, 4)):
            rights += rotate(xbuf[i + offset, 0], xbuf[i + offset, 1], lanes, d, i, 1)
        acc[i] += pair_products(left, rights)

    def wide(slot, part, lanes):
        return jnp.concatenate([buf[slot, part, comp, :, lanes] for comp in range(3)], axis=1)

    def block_step(i, block):
        lanes = lanes_of(block)
        left = jnp.concatenate([wide(i, 0, lanes), wide(i, 1, lanes)], axis=0)
        rights = []
        for d, offset in enumerate((1, 4)):
            rights += rotate(wide(i + offset, 0, lanes), wide(i + offset, 1, lanes), lanes, d, i, 3)
        acc[i] += pair_products(left, rights)

    lane32 = lax.broadcasted_iota(jnp.int32, (32, LANES), 1)
    lane16 = lax.broadcasted_iota(jnp.int32, (16, LANES), 1)
    holder = core * 4 + zpos
    spans = [(0, 2)] + [(0, 3)] * 3 + [(0, 4)] * 4 + [(2, 2)] + [(3, 1)] * 3

    def target_copy(i):
        part = pl.ds(*spans[i])
        target = (first_k + i + 32) % 32
        return target, pltpu.make_async_remote_copy(
            src_ref=stage.at[i, part], dst_ref=reduced.at[holder, part],
            send_sem=rsend_sem.at[i], recv_sem=rrecv_sem,
            device_id={"ka": target}, device_id_type=MESH,
        )

    def send_target(i):
        part = pl.ds(*spans[i])
        target, copy = target_copy(i)

        @pl.when(target == me)
        def _():
            pltpu.make_async_copy(stage.at[i, part], reduced.at[holder, part], rrecv_sem).start()

        @pl.when(target != me)
        def _():
            copy.start()

    def finish_matrices(i):
        top = acc[i, pl.ds(0, 32), :]
        bottom = acc[i, pl.ds(32, 32), :]
        swapped = jnp.where(
            lane32 % 64 < 32, pltpu.roll(bottom, 96, 1), -pltpu.roll(bottom, 32, 1)
        )
        value = top + swapped
        turned = pltpu.roll(value, 64, 1)
        along_x = jnp.where(lane16 < 64, value[:16], turned[16:])
        along_y = jnp.where(lane16 < 64, turned[:16], value[16:])
        stage[i, 0] = along_x
        stage[i, 1] = along_y
        stage[i + 1, 2] = along_x
        stage[i + 4, 3] = along_y

    for n, block in late:
        for e, other in early:
            if block[0] <= other[0] < block[0] + block[1]:
                wait_block(2 - 2 * core, other, passed_sem.at[e])
        wait_block(1, block, late_sem.at[n])
        for i in range(ROW):
            block_step(i, block)
    pl.semaphore_wait(across_sem.at[1], 1)
    pl.semaphore_wait(rows_sem, 2)
    wait_extra(2 - 2 * core)
    wait_extra(1)
    for i in range(ROW):
        extra_step(i)
        finish_matrices(i)
    for i in range(SLOTS):
        send_target(i)

    def slab_copy(dx):
        return pltpu.make_async_remote_copy(
            src_ref=total, dst_ref=gathered.at[gx],
            send_sem=gsend_sem.at[dx - 1], recv_sem=grecv_sem,
            device_id={"gz": (gx + dx) % 4}, device_id_type=MESH,
        )

    pltpu.make_async_copy(reduced, reduced, rrecv_sem).wait()
    value = reduced[0]
    for j in range(1, ROW):
        value = value + reduced[j]
    total[...] = value
    for dx in (2, 1, 3):
        slab_copy(dx).start()
    gathered[gx] = value

    seven = xbuf.at[pl.ds(0, 7)]
    pltpu.make_async_copy(seven, seven, xsend_sem).wait()
    pass_extra.wait_send()

    sent = buf.at[pl.ds(0, 7)]
    pltpu.make_async_copy(sent, sent, send_sem).wait()
    for n, block in early:
        pass_block(n, block).wait_send()
    for i in range(SLOTS):
        target, copy = target_copy(i)

        @pl.when(target != me)
        def _():
            copy.wait_send()

    block = gathered.at[pl.ds(0, 3)]
    pltpu.make_async_copy(block, block, grecv_sem).wait()
    summed = gathered[0] + gathered[1] + gathered[2] + gathered[3]
    for index, direction in ((0, 0), (1, 2), (2, 1), (3, 3)):
        value = summed[index]
        real = jnp.concatenate([value[:, 0:32], value[:, 64:96]], axis=0)
        imag = jnp.concatenate([value[:, 32:64], value[:, 96:128]], axis=0)
        if index < 2:
            out_ref[direction, 0] = real
            out_ref[direction, 1] = imag
        else:
            out_ref[direction, 0] = real.T
            out_ref[direction, 1] = -imag.T
    for dx in (1, 2, 3):
        slab_copy(dx).wait_send()


def per_device(fields, bvectors, gshift):
    local, vectors, shifts = (
        pltpu.with_memory_space_constraint(value, pltpu.HBM)
        for value in (
            jnp.transpose(fields[0], (0, 2, 1, 3)), bvectors, jnp.transpose(gshift, (2, 1, 0))
        )
    )
    dma = pltpu.SemaphoreType.DMA
    f32 = jnp.float32
    result = pl.pallas_call(
        kernel,
        out_shape=jax.ShapeDtypeStruct((4, 2, 32, 32), f32),
        in_specs=[
            pl.BlockSpec(memory_space=pltpu.HBM),
            pl.BlockSpec(memory_space=pltpu.HBM),
            pl.BlockSpec(memory_space=pltpu.HBM),
        ],
        out_specs=pl.BlockSpec(memory_space=pltpu.VMEM),
        scratch_shapes=[
            pltpu.SMEM((2, 3), f32),
            pltpu.SMEM((3, 2, 32), jnp.int32),
            pltpu.VMEM((SLOTS, 2, 3, 32, TILES * LANES), f32),
            pltpu.VMEM((SLOTS, 2, 32, LANES), f32),
            pltpu.VMEM((2, 16, (TILES + 1) * LANES), f32),
            pltpu.VMEM((ROW, 64, LANES), f32),
            pltpu.VMEM((SLOTS, 4, 16, LANES), f32),
            pltpu.VMEM((ROW, 4, 16, LANES), f32),
            pltpu.VMEM((4, 16, LANES), f32),
            pltpu.VMEM((4, 4, 16, LANES), f32),
            dma((2,)),
            dma,
            dma((len(EARLY),)),
            dma((len(LATE),)),
            dma((len(EARLY),)),
            dma,
            dma((3,)),
            dma((len(EARLY),)),
            dma,
            dma((SLOTS,)),
            dma,
            dma((3,)),
            dma,
            pltpu.SemaphoreType.REGULAR,
            pltpu.SemaphoreType.REGULAR((2,)),
        ],
        compiler_params=pltpu.CompilerParams(
            collective_id=0, has_side_effects=True, vmem_limit_bytes=40000 * 1024
        ),
        name="wannier",
    )(vectors, shifts, local)
    return result[None]


def solution(mesh):
    in_specs = (P("ka", None, None, None, "gz"), P(), P())
    out_specs = P("ka", None, None, None, None)
    return jax.shard_map(
        per_device, mesh=mesh, in_specs=in_specs, out_specs=out_specs, check_vma=False
    )
```

```python
import math

import jax
import jax.numpy as jnp
from jax import lax
from jax.experimental import pallas as pl
from jax.experimental.pallas import tpu as pltpu
from jax.sharding import PartitionSpec as P

GX = 40
GY = 40
NZ = 16
ROW = 8
ROWS = 4
SLOTS = 12
TILES = 6
LANES = 128
EARLY = ((0, 2), (2, 2), (4, 2))
LATE = ((0, 2), (2, 2), (4, 1), (5, 1))
MESH = pl.DeviceIdType.MESH
TWO_PI = 2.0 * math.pi


def split(value):
    high = value.astype(jnp.bfloat16)
    low = (value - high.astype(jnp.float32)).astype(jnp.bfloat16)
    return high, low


def contract(left, right):
    return lax.dot_general(
        left, right, (((1,), (1,)), ((), ())), preferred_element_type=jnp.float32
    )


def kernel(
    bvec_hbm, gshift_hbm, field_ref, out_ref,
    bvec_ref, gshift_ref, local, buf, xbuf, phase, acc, stage, reduced, total, gathered,
    small_sem, load_sem, send_sem, early_sem, late_sem, passed_sem, xsend_sem, xrecv_sem, fsend_sem, xfsend_sem,
    rsend_sem, rrecv_sem, gsend_sem, grecv_sem, rows_sem, across_sem,
):
    me = lax.axis_index("ka")
    gx = lax.axis_index("gz")
    row = me // ROW
    own = me % ROW
    zpos = own // 2
    core = own % 2
    side = zpos // 2
    row_up = (row + 1) % ROWS
    row_down = (row + ROWS - 1) % ROWS
    pass_row = jnp.where(core == 0, row_down, row_up)
    pass_from = 8 * core
    pass_to = 8 - 8 * core
    first_k = row * ROW - 4 * core

    def at(r, j):
        return {"ka": r * ROW + j}

    sibling = zpos * 2 + 1 - core
    others = [((zpos + dz) % 4) * 2 for dz in (1, 3, 2)]
    barrier = pltpu.get_barrier_semaphore()
    near = [at(row, z + c) for z in others[:2] for c in range(2)] + [at(row, sibling)]
    near += [at(row_up, own), at(row_down, own)]
    near += [{"gz": (gx + 1) % 4}, {"gz": (gx + 3) % 4}]
    for device in near:
        pl.semaphore_signal(barrier, inc=1, device_id=device, device_id_type=MESH)
    small = [
        pltpu.make_async_copy(bvec_hbm, bvec_ref, small_sem.at[0]),
        pltpu.make_async_copy(gshift_hbm, gshift_ref, small_sem.at[1]),
    ]
    for copy in small:
        copy.start()


    def load(p):
        part = pl.ds(pl.multiple_of(p * TILES * LANES, LANES), TILES * LANES)
        return pltpu.make_async_copy(
            field_ref.at[:, :, :, part], local.at[:, :, :, part], load_sem.at[p]
        )

    odd = pl.ds(ROW * TILES * LANES, 2 * LANES)
    load_odd = pltpu.make_async_copy(
        field_ref.at[:, :, :, odd], local.at[:, :, :, odd], load_sem.at[ROW]
    )
    load_odd.start()
    for c in (side, 1 - side):
        for z in others:
            load(z + c).start()
    load(sibling).start()
    pl.semaphore_wait(barrier, len(near))
    pl.semaphore_signal(across_sem.at[0], inc=1, device_id=at(row, others[1] + core), device_id_type=MESH)
    pl.semaphore_signal(across_sem.at[1], inc=1, device_id={"gz": (gx + 3) % 4}, device_id_type=MESH)

    def extra_source(source, p):
        comp = jnp.minimum(p // 2, 2)
        start = pl.multiple_of((ROW * TILES + p % 2) * LANES, LANES)
        return source.at[:, comp, :, pl.ds(start, LANES)]

    def lanes_of(block):
        return pl.ds(block[0] * LANES, block[1] * LANES)

    def block_source(source, p, block):
        start = pl.multiple_of((p * TILES + block[0]) * LANES, LANES)
        return source.at[:, :, :, pl.ds(start, block[1] * LANES)]

    def block_target(slot, block):
        return buf.at[slot, :, :, :, lanes_of(block)]

    def send_extra(z, c):
        pltpu.make_async_remote_copy(
            src_ref=extra_source(local, z + c), dst_ref=xbuf.at[own + 4 * c],
            send_sem=xsend_sem, recv_sem=xrecv_sem.at[side + c],
            device_id=at(row, z + c), device_id_type=MESH,
        ).start()

    def keep_extra(c):
        pltpu.make_async_copy(
            extra_source(field_ref, own), xbuf.at[own + 4 * c], xrecv_sem.at[side + c]
        ).start()

    def send_blocks(z, c, blocks, sems):
        for n, block in blocks:
            pltpu.make_async_remote_copy(
                src_ref=block_source(local, z + c, block), dst_ref=block_target(own + 4 * c, block),
                send_sem=send_sem, recv_sem=sems.at[n],
                device_id=at(row, z + c), device_id_type=MESH,
            ).start()

    def keep_blocks(c, blocks, sems):
        for n, block in blocks:
            pltpu.make_async_copy(
                block_source(field_ref, own, block), block_target(own + 4 * c, block), sems.at[n]
            ).start()

    early = list(enumerate(EARLY))
    late = list(enumerate(LATE))
    for z in others[:2]:
        load(z + side).wait()
        send_blocks(z, side, early[:1], early_sem)
    load_odd.wait()
    for z in others[:2]:
        send_extra(z, side)
    load(others[2] + side).wait()
    pl.semaphore_wait(across_sem.at[0], 1)
    send_extra(others[2], side)
    send_blocks(others[2], side, early[:1], early_sem)
    for pair in early[1:]:
        for z in others:
            send_blocks(z, side, [pair], early_sem)
    here = zpos * 2
    load(sibling).wait()

    @pl.when(core == side)
    def _():
        keep_extra(side)
        keep_blocks(side, early, early_sem)
        send_extra(here, 1 - side)
        send_blocks(here, 1 - side, late, late_sem)

    @pl.when(core != side)
    def _():
        send_extra(here, side)
        send_blocks(here, side, early, early_sem)
        keep_extra(1 - side)
        keep_blocks(1 - side, late, late_sem)

    for z in others:
        load(z + 1 - side).wait()
    for pair in late:
        for z in others:
            send_blocks(z, 1 - side, [pair], late_sem)
    for z in others:
        send_extra(z, 1 - side)

    for r in (row_up, row_down):
        pl.semaphore_signal(rows_sem, inc=1, device_id=at(r, own), device_id_type=MESH)

    for copy in small:
        copy.wait()

    row_id = lax.broadcasted_iota(jnp.int32, (16, LANES), 0)
    lane = lax.broadcasted_iota(jnp.int32, (16, TILES * LANES), 1).astype(jnp.float32)
    q = []
    for a in range(3):
        values = jnp.zeros((16, LANES), jnp.float32)
        for d in range(2):
            for i in range(8):
                k = (first_k + i + 32) % 32
                value = bvec_ref[d, a] + gshift_ref[a, d, k].astype(jnp.float32)
                values = jnp.where(row_id == d * 8 + i, value, values)
        q.append(jnp.concatenate([values] * TILES, axis=1))

    def phases_of(start, width):
        cell = lane[:, :width] + start.astype(jnp.float32)
        line = jnp.floor((cell + 0.5) * (1.0 / GX))
        plane = jnp.floor((cell + 0.5) * (1.0 / (GX * GY)))
        xc = cell - GX * line
        yc = line - GY * plane
        zc = plane + (gx * 4).astype(jnp.float32)
        q0, q1, q2 = (values[:, :width] for values in q)
        theta = -TWO_PI * (q0 * xc / GX + q1 * yc / GY + q2 * zc / NZ)
        return jnp.cos(theta), jnp.sin(theta)

    cosine, sine = phases_of(own * TILES * LANES, TILES * LANES)
    phase[0, :, pl.ds(0, TILES * LANES)] = cosine
    phase[1, :, pl.ds(0, TILES * LANES)] = sine
    cosine, sine = phases_of((ROW * TILES + own % 2) * LANES, LANES)
    keep = (own < 6).astype(jnp.float32)
    phase[0, :, pl.ds(TILES * LANES, LANES)] = cosine * keep
    phase[1, :, pl.ds(TILES * LANES, LANES)] = sine * keep
    acc[...] = jnp.zeros_like(acc)

    def wait_block(group, block, sem):
        target = block_target(pl.ds(4 * group, 4), block)
        pltpu.make_async_copy(target, target, sem).wait()

    def wait_extra(group):
        block = xbuf.at[pl.ds(4 * group, 4)]
        pltpu.make_async_copy(block, block, xrecv_sem.at[group]).wait()

    pass_extra = pltpu.make_async_remote_copy(
        src_ref=xbuf.at[pl.ds(pass_from, 4)], dst_ref=xbuf.at[pl.ds(pass_to, 4)],
        send_sem=xfsend_sem, recv_sem=xrecv_sem.at[2 - 2 * core],
        device_id=at(pass_row, own), device_id_type=MESH,
    )

    def pass_block(n, block):
        return pltpu.make_async_remote_copy(
            src_ref=block_target(pl.ds(pass_from, 4), block),
            dst_ref=block_target(pl.ds(pass_to, 4), block),
            send_sem=fsend_sem.at[n], recv_sem=passed_sem.at[n],
            device_id=at(pass_row, own), device_id_type=MESH,
        )

    wait_extra(2 * core)
    pass_extra.start()
    for n, block in early:
        wait_block(2 * core, block, early_sem.at[n])
        pass_block(n, block).start()

    def pair_products(left, rights):
        left_high, left_low = split(left)
        right_high, right_low = split(jnp.concatenate(rights, axis=0))
        return (
            contract(left_high, right_high)
            + contract(left_high, right_low)
            + contract(left_low, right_high)
        )

    def rotate(real, imag, lanes, d, i, comps):
        c = phase[0, pl.ds(d * 8 + i, 1), lanes]
        s = phase[1, pl.ds(d * 8 + i, 1), lanes]
        width = c.shape[1]
        c = jnp.concatenate([jnp.broadcast_to(c, (32, width))] * comps, axis=1)
        s = jnp.concatenate([jnp.broadcast_to(s, (32, width))] * comps, axis=1)
        return [c * real - s * imag, s * real + c * imag]

    def extra_step(i):
        left = xbuf[i].reshape(64, LANES)
        lanes = pl.ds(TILES * LANES, LANES)
        rights = []
        for d, offset in enumerate((1, 4)):
            rights += rotate(xbuf[i + offset, 0], xbuf[i + offset, 1], lanes, d, i, 1)
        acc[i] += pair_products(left, rights)

    def wide(slot, part, lanes):
        return jnp.concatenate([buf[slot, part, comp, :, lanes] for comp in range(3)], axis=1)

    def block_step(i, block):
        lanes = lanes_of(block)
        left = jnp.concatenate([wide(i, 0, lanes), wide(i, 1, lanes)], axis=0)
        rights = []
        for d, offset in enumerate((1, 4)):
            rights += rotate(wide(i + offset, 0, lanes), wide(i + offset, 1, lanes), lanes, d, i, 3)
        acc[i] += pair_products(left, rights)

    lane32 = lax.broadcasted_iota(jnp.int32, (32, LANES), 1)
    lane16 = lax.broadcasted_iota(jnp.int32, (16, LANES), 1)
    holder = core * 4 + zpos
    spans = [(0, 2)] + [(0, 3)] * 3 + [(0, 4)] * 4 + [(2, 2)] + [(3, 1)] * 3

    def target_copy(i):
        part = pl.ds(*spans[i])
        target = (first_k + i + 32) % 32
        return target, pltpu.make_async_remote_copy(
            src_ref=stage.at[i, part], dst_ref=reduced.at[holder, part],
            send_sem=rsend_sem.at[i], recv_sem=rrecv_sem,
            device_id={"ka": target}, device_id_type=MESH,
        )

    def send_target(i):
        part = pl.ds(*spans[i])
        target, copy = target_copy(i)

        @pl.when(target == me)
        def _():
            pltpu.make_async_copy(stage.at[i, part], reduced.at[holder, part], rrecv_sem).start()

        @pl.when(target != me)
        def _():
            copy.start()

    def finish_matrices(i):
        top = acc[i, pl.ds(0, 32), :]
        bottom = acc[i, pl.ds(32, 32), :]
        swapped = jnp.where(
            lane32 % 64 < 32, pltpu.roll(bottom, 96, 1), -pltpu.roll(bottom, 32, 1)
        )
        value = top + swapped
        turned = pltpu.roll(value, 64, 1)
        along_x = jnp.where(lane16 < 64, value[:16], turned[16:])
        along_y = jnp.where(lane16 < 64, turned[:16], value[16:])
        stage[i, 0] = along_x
        stage[i, 1] = along_y
        stage[i + 1, 2] = along_x
        stage[i + 4, 3] = along_y

    for n, block in late:
        for e, other in early:
            if block[0] <= other[0] < block[0] + block[1]:
                wait_block(2 - 2 * core, other, passed_sem.at[e])
        wait_block(1, block, late_sem.at[n])
        for i in range(ROW):
            block_step(i, block)
    pl.semaphore_wait(across_sem.at[1], 1)
    pl.semaphore_wait(rows_sem, 2)
    wait_extra(2 - 2 * core)
    wait_extra(1)
    for i in range(ROW):
        extra_step(i)
        finish_matrices(i)
    for i in range(SLOTS):
        send_target(i)

    def slab_copy(dx):
        return pltpu.make_async_remote_copy(
            src_ref=total, dst_ref=gathered.at[gx],
            send_sem=gsend_sem.at[dx - 1], recv_sem=grecv_sem,
            device_id={"gz": (gx + dx) % 4}, device_id_type=MESH,
        )

    pltpu.make_async_copy(reduced, reduced, rrecv_sem).wait()
    value = reduced[0]
    for j in range(1, ROW):
        value = value + reduced[j]
    total[...] = value
    for dx in (2, 1, 3):
        slab_copy(dx).start()
    gathered[gx] = value

    seven = xbuf.at[pl.ds(0, 7)]
    pltpu.make_async_copy(seven, seven, xsend_sem).wait()
    pass_extra.wait_send()

    sent = buf.at[pl.ds(0, 7)]
    pltpu.make_async_copy(sent, sent, send_sem).wait()
    for n, block in early:
        pass_block(n, block).wait_send()
    for i in range(SLOTS):
        target, copy = target_copy(i)

        @pl.when(target != me)
        def _():
            copy.wait_send()

    block = gathered.at[pl.ds(0, 3)]
    pltpu.make_async_copy(block, block, grecv_sem).wait()
    summed = gathered[0] + gathered[1] + gathered[2] + gathered[3]
    for index, direction in ((0, 0), (1, 2), (2, 1), (3, 3)):
        value = summed[index]
        real = jnp.concatenate([value[:, 0:32], value[:, 64:96]], axis=0)
        imag = jnp.concatenate([value[:, 32:64], value[:, 96:128]], axis=0)
        if index < 2:
            out_ref[direction, 0] = real
            out_ref[direction, 1] = imag
        else:
            out_ref[direction, 0] = real.T
            out_ref[direction, 1] = -imag.T
    for dx in (1, 2, 3):
        slab_copy(dx).wait_send()


def per_device(fields, bvectors, gshift):
    local, vectors, shifts = (
        pltpu.with_memory_space_constraint(value, pltpu.HBM)
        for value in (
            jnp.transpose(fields[0], (0, 2, 1, 3)), bvectors, jnp.transpose(gshift, (2, 1, 0))
        )
    )
    dma = pltpu.SemaphoreType.DMA
    f32 = jnp.float32
    result = pl.pallas_call(
        kernel,
        out_shape=jax.ShapeDtypeStruct((4, 2, 32, 32), f32),
        in_specs=[
            pl.BlockSpec(memory_space=pltpu.HBM),
            pl.BlockSpec(memory_space=pltpu.HBM),
            pl.BlockSpec(memory_space=pltpu.HBM),
        ],
        out_specs=pl.BlockSpec(memory_space=pltpu.VMEM),
        scratch_shapes=[
            pltpu.SMEM((2, 3), f32),
            pltpu.SMEM((3, 2, 32), jnp.int32),
            pltpu.VMEM((2, 3, 32, GX * GY * NZ // 4), f32),
            pltpu.VMEM((SLOTS, 2, 3, 32, TILES * LANES), f32),
            pltpu.VMEM((SLOTS, 2, 32, LANES), f32),
            pltpu.VMEM((2, 16, (TILES + 1) * LANES), f32),
            pltpu.VMEM((ROW, 64, LANES), f32),
            pltpu.VMEM((SLOTS, 4, 16, LANES), f32),
            pltpu.VMEM((ROW, 4, 16, LANES), f32),
            pltpu.VMEM((4, 16, LANES), f32),
            pltpu.VMEM((4, 4, 16, LANES), f32),
            dma((2,)),
            dma((ROW + 1,)),
            dma,
            dma((len(EARLY),)),
            dma((len(LATE),)),
            dma((len(EARLY),)),
            dma,
            dma((3,)),
            dma((len(EARLY),)),
            dma,
            dma((SLOTS,)),
            dma,
            dma((3,)),
            dma,
            pltpu.SemaphoreType.REGULAR,
            pltpu.SemaphoreType.REGULAR((2,)),
        ],
        compiler_params=pltpu.CompilerParams(
            collective_id=0, has_side_effects=True, vmem_limit_bytes=40000 * 1024
        ),
        name="wannier",
    )(vectors, shifts, local)
    return result[None]


def solution(mesh):
    in_specs = (P("ka", None, None, None, "gz"), P(), P())
    out_specs = P("ka", None, None, None, None)
    return jax.shard_map(
        per_device, mesh=mesh, in_specs=in_specs, out_specs=out_specs, check_vma=False
    )
```

```python
import math

import jax
import jax.numpy as jnp
from jax import lax
from jax.experimental import pallas as pl
from jax.experimental.pallas import tpu as pltpu
from jax.sharding import PartitionSpec as P

GX = 40
GY = 40
NZ = 16
ROW = 8
ROWS = 4
SLOTS = 12
TILES = 6
LANES = 128
EARLY = ((0, 2), (2, 2), (4, 2))
LATE = ((0, 2), (2, 2), (4, 1), (5, 1))
MESH = pl.DeviceIdType.MESH
TWO_PI = 2.0 * math.pi


def split(value):
    high = value.astype(jnp.bfloat16)
    low = (value - high.astype(jnp.float32)).astype(jnp.bfloat16)
    return high, low


def contract(left, right):
    return lax.dot_general(
        left, right, (((1,), (1,)), ((), ())), preferred_element_type=jnp.float32
    )


def kernel(
    bvec_hbm, gshift_hbm, field_ref, out_ref,
    bvec_ref, gshift_ref, buf, xbuf, phase, acc, stage, reduced, total, gathered,
    small_sem, send_sem, early_sem, late_sem, passed_sem, xsend_sem, xrecv_sem, fsend_sem, xfsend_sem,
    rsend_sem, rrecv_sem, gsend_sem, grecv_sem, rows_sem, across_sem,
):
    me = lax.axis_index("ka")
    gx = lax.axis_index("gz")
    row = me // ROW
    own = me % ROW
    zpos = own // 2
    core = own % 2
    side = zpos // 2
    row_up = (row + 1) % ROWS
    row_down = (row + ROWS - 1) % ROWS
    pass_row = jnp.where(core == 0, row_down, row_up)
    pass_from = 8 * core
    pass_to = 8 - 8 * core
    first_k = row * ROW - 4 * core

    def at(r, j):
        return {"ka": r * ROW + j}

    sibling = zpos * 2 + 1 - core
    others = [((zpos + dz) % 4) * 2 for dz in (1, 3, 2)]
    barrier = pltpu.get_barrier_semaphore()
    near = [at(row, z + c) for z in others[:2] for c in range(2)] + [at(row, sibling)]
    near += [at(row_up, own), at(row_down, own)]
    near += [{"gz": (gx + 1) % 4}, {"gz": (gx + 3) % 4}]
    for device in near:
        pl.semaphore_signal(barrier, inc=1, device_id=device, device_id_type=MESH)
    small = [
        pltpu.make_async_copy(bvec_hbm, bvec_ref, small_sem.at[0]),
        pltpu.make_async_copy(gshift_hbm, gshift_ref, small_sem.at[1]),
    ]
    for copy in small:
        copy.start()

    pl.semaphore_wait(barrier, len(near))
    pl.semaphore_signal(across_sem.at[0], inc=1, device_id=at(row, others[1] + core), device_id_type=MESH)
    pl.semaphore_signal(across_sem.at[1], inc=1, device_id={"gz": (gx + 3) % 4}, device_id_type=MESH)

    def extra_source(p):
        comp = jnp.minimum(p // 2, 2)
        start = pl.multiple_of((ROW * TILES + p % 2) * LANES, LANES)
        return field_ref.at[:, comp, :, pl.ds(start, LANES)]

    def lanes_of(block):
        return pl.ds(block[0] * LANES, block[1] * LANES)

    def block_source(p, block):
        start = pl.multiple_of((p * TILES + block[0]) * LANES, LANES)
        return field_ref.at[:, :, :, pl.ds(start, block[1] * LANES)]

    def block_target(slot, block):
        return buf.at[slot, :, :, :, lanes_of(block)]

    def send_extra(z, c):
        pltpu.make_async_remote_copy(
            src_ref=extra_source(z + c), dst_ref=xbuf.at[own + 4 * c],
            send_sem=xsend_sem, recv_sem=xrecv_sem.at[side + c],
            device_id=at(row, z + c), device_id_type=MESH,
        ).start()

    def keep_extra(c):
        pltpu.make_async_copy(
            extra_source(own), xbuf.at[own + 4 * c], xrecv_sem.at[side + c]
        ).start()

    def send_blocks(z, c, blocks, sems):
        for n, block in blocks:
            pltpu.make_async_remote_copy(
                src_ref=block_source(z + c, block), dst_ref=block_target(own + 4 * c, block),
                send_sem=send_sem, recv_sem=sems.at[n],
                device_id=at(row, z + c), device_id_type=MESH,
            ).start()

    def keep_blocks(c, blocks, sems):
        for n, block in blocks:
            pltpu.make_async_copy(
                block_source(own, block), block_target(own + 4 * c, block), sems.at[n]
            ).start()

    early = list(enumerate(EARLY))
    late = list(enumerate(LATE))
    for z in others[:2]:
        send_extra(z, side)
    for z in others[:2]:
        send_blocks(z, side, early[:1], early_sem)
    pl.semaphore_wait(across_sem.at[0], 1)
    send_extra(others[2], side)
    send_blocks(others[2], side, early[:1], early_sem)
    for pair in early[1:]:
        for z in others:
            send_blocks(z, side, [pair], early_sem)
    here = zpos * 2

    @pl.when(core == side)
    def _():
        keep_extra(side)
        keep_blocks(side, early, early_sem)
        send_extra(here, 1 - side)
        send_blocks(here, 1 - side, late, late_sem)

    @pl.when(core != side)
    def _():
        send_extra(here, side)
        send_blocks(here, side, early, early_sem)
        keep_extra(1 - side)
        keep_blocks(1 - side, late, late_sem)

    for pair in late:
        for z in others:
            send_blocks(z, 1 - side, [pair], late_sem)
    for z in others:
        send_extra(z, 1 - side)

    for r in (row_up, row_down):
        pl.semaphore_signal(rows_sem, inc=1, device_id=at(r, own), device_id_type=MESH)

    for copy in small:
        copy.wait()

    row_id = lax.broadcasted_iota(jnp.int32, (16, LANES), 0)
    lane = lax.broadcasted_iota(jnp.int32, (16, TILES * LANES), 1).astype(jnp.float32)
    q = []
    for a in range(3):
        values = jnp.zeros((16, LANES), jnp.float32)
        for d in range(2):
            for i in range(8):
                k = (first_k + i + 32) % 32
                value = bvec_ref[d, a] + gshift_ref[a, d, k].astype(jnp.float32)
                values = jnp.where(row_id == d * 8 + i, value, values)
        q.append(jnp.concatenate([values] * TILES, axis=1))

    def phases_of(start, width):
        cell = lane[:, :width] + start.astype(jnp.float32)
        line = jnp.floor((cell + 0.5) * (1.0 / GX))
        plane = jnp.floor((cell + 0.5) * (1.0 / (GX * GY)))
        xc = cell - GX * line
        yc = line - GY * plane
        zc = plane + (gx * 4).astype(jnp.float32)
        q0, q1, q2 = (values[:, :width] for values in q)
        theta = -TWO_PI * (q0 * xc / GX + q1 * yc / GY + q2 * zc / NZ)
        return jnp.cos(theta), jnp.sin(theta)

    cosine, sine = phases_of(own * TILES * LANES, TILES * LANES)
    phase[0, :, pl.ds(0, TILES * LANES)] = cosine
    phase[1, :, pl.ds(0, TILES * LANES)] = sine
    cosine, sine = phases_of((ROW * TILES + own % 2) * LANES, LANES)
    keep = (own < 6).astype(jnp.float32)
    phase[0, :, pl.ds(TILES * LANES, LANES)] = cosine * keep
    phase[1, :, pl.ds(TILES * LANES, LANES)] = sine * keep
    acc[...] = jnp.zeros_like(acc)

    def wait_block(group, block, sem):
        target = block_target(pl.ds(4 * group, 4), block)
        pltpu.make_async_copy(target, target, sem).wait()

    def wait_extra(group):
        block = xbuf.at[pl.ds(4 * group, 4)]
        pltpu.make_async_copy(block, block, xrecv_sem.at[group]).wait()

    pass_extra = pltpu.make_async_remote_copy(
        src_ref=xbuf.at[pl.ds(pass_from, 4)], dst_ref=xbuf.at[pl.ds(pass_to, 4)],
        send_sem=xfsend_sem, recv_sem=xrecv_sem.at[2 - 2 * core],
        device_id=at(pass_row, own), device_id_type=MESH,
    )

    def pass_block(n, block):
        return pltpu.make_async_remote_copy(
            src_ref=block_target(pl.ds(pass_from, 4), block),
            dst_ref=block_target(pl.ds(pass_to, 4), block),
            send_sem=fsend_sem.at[n], recv_sem=passed_sem.at[n],
            device_id=at(pass_row, own), device_id_type=MESH,
        )

    wait_extra(2 * core)
    pass_extra.start()
    for n, block in early:
        wait_block(2 * core, block, early_sem.at[n])
        pass_block(n, block).start()

    def pair_products(left, rights):
        left_high, left_low = split(left)
        right_high, right_low = split(jnp.concatenate(rights, axis=0))
        both = contract(
            jnp.concatenate([left_high, left_low], axis=0),
            jnp.concatenate([right_high, right_low], axis=0),
        )
        return both[:64, :128] + both[64:, :128] + both[:64, 128:]

    def rotate(real, imag, lanes, d, i, comps):
        c = phase[0, pl.ds(d * 8 + i, 1), lanes]
        s = phase[1, pl.ds(d * 8 + i, 1), lanes]
        width = c.shape[1]
        c = jnp.concatenate([jnp.broadcast_to(c, (32, width))] * comps, axis=1)
        s = jnp.concatenate([jnp.broadcast_to(s, (32, width))] * comps, axis=1)
        return [c * real - s * imag, s * real + c * imag]

    def extra_step(i):
        left = xbuf[i].reshape(64, LANES)
        lanes = pl.ds(TILES * LANES, LANES)
        rights = []
        for d, offset in enumerate((1, 4)):
            rights += rotate(xbuf[i + offset, 0], xbuf[i + offset, 1], lanes, d, i, 1)
        acc[i] += pair_products(left, rights)

    def wide(slot, part, lanes):
        return jnp.concatenate([buf[slot, part, comp, :, lanes] for comp in range(3)], axis=1)

    def block_step(i, block):
        lanes = lanes_of(block)
        left = jnp.concatenate([wide(i, 0, lanes), wide(i, 1, lanes)], axis=0)
        rights = []
        for d, offset in enumerate((1, 4)):
            rights += rotate(wide(i + offset, 0, lanes), wide(i + offset, 1, lanes), lanes, d, i, 3)
        acc[i] += pair_products(left, rights)

    lane32 = lax.broadcasted_iota(jnp.int32, (32, LANES), 1)
    lane16 = lax.broadcasted_iota(jnp.int32, (16, LANES), 1)
    holder = core * 4 + zpos
    spans = [(0, 2)] + [(0, 3)] * 3 + [(0, 4)] * 4 + [(2, 2)] + [(3, 1)] * 3

    def target_copy(i):
        part = pl.ds(*spans[i])
        target = (first_k + i + 32) % 32
        return target, pltpu.make_async_remote_copy(
            src_ref=stage.at[i, part], dst_ref=reduced.at[holder, part],
            send_sem=rsend_sem.at[i], recv_sem=rrecv_sem,
            device_id={"ka": target}, device_id_type=MESH,
        )

    def send_target(i):
        part = pl.ds(*spans[i])
        target, copy = target_copy(i)

        @pl.when(target == me)
        def _():
            pltpu.make_async_copy(stage.at[i, part], reduced.at[holder, part], rrecv_sem).start()

        @pl.when(target != me)
        def _():
            copy.start()

    def finish_matrices(i):
        top = acc[i, pl.ds(0, 32), :]
        bottom = acc[i, pl.ds(32, 32), :]
        swapped = jnp.where(
            lane32 % 64 < 32, pltpu.roll(bottom, 96, 1), -pltpu.roll(bottom, 32, 1)
        )
        value = top + swapped
        turned = pltpu.roll(value, 64, 1)
        along_x = jnp.where(lane16 < 64, value[:16], turned[16:])
        along_y = jnp.where(lane16 < 64, turned[:16], value[16:])
        stage[i, 0] = along_x
        stage[i, 1] = along_y
        stage[i + 1, 2] = along_x
        stage[i + 4, 3] = along_y

    for n, block in late:
        for e, other in early:
            if block[0] <= other[0] < block[0] + block[1]:
                wait_block(2 - 2 * core, other, passed_sem.at[e])
        wait_block(1, block, late_sem.at[n])
        for i in range(ROW):
            block_step(i, block)
    pl.semaphore_wait(across_sem.at[1], 1)
    pl.semaphore_wait(rows_sem, 2)
    wait_extra(2 - 2 * core)
    wait_extra(1)
    for i in range(ROW):
        extra_step(i)
        finish_matrices(i)
    for i in range(SLOTS):
        send_target(i)

    def slab_copy(dx):
        return pltpu.make_async_remote_copy(
            src_ref=total, dst_ref=gathered.at[gx],
            send_sem=gsend_sem.at[dx - 1], recv_sem=grecv_sem,
            device_id={"gz": (gx + dx) % 4}, device_id_type=MESH,
        )

    pltpu.make_async_copy(reduced, reduced, rrecv_sem).wait()
    value = reduced[0]
    for j in range(1, ROW):
        value = value + reduced[j]
    total[...] = value
    for dx in (2, 1, 3):
        slab_copy(dx).start()
    gathered[gx] = value

    seven = xbuf.at[pl.ds(0, 7)]
    pltpu.make_async_copy(seven, seven, xsend_sem).wait()
    pass_extra.wait_send()

    sent = buf.at[pl.ds(0, 7)]
    pltpu.make_async_copy(sent, sent, send_sem).wait()
    for n, block in early:
        pass_block(n, block).wait_send()
    for i in range(SLOTS):
        target, copy = target_copy(i)

        @pl.when(target != me)
        def _():
            copy.wait_send()

    block = gathered.at[pl.ds(0, 3)]
    pltpu.make_async_copy(block, block, grecv_sem).wait()
    summed = gathered[0] + gathered[1] + gathered[2] + gathered[3]
    for index, direction in ((0, 0), (1, 2), (2, 1), (3, 3)):
        value = summed[index]
        real = jnp.concatenate([value[:, 0:32], value[:, 64:96]], axis=0)
        imag = jnp.concatenate([value[:, 32:64], value[:, 96:128]], axis=0)
        if index < 2:
            out_ref[direction, 0] = real
            out_ref[direction, 1] = imag
        else:
            out_ref[direction, 0] = real.T
            out_ref[direction, 1] = -imag.T
    for dx in (1, 2, 3):
        slab_copy(dx).wait_send()


def per_device(fields, bvectors, gshift):
    local, vectors, shifts = (
        pltpu.with_memory_space_constraint(value, pltpu.HBM)
        for value in (
            jnp.transpose(fields[0], (0, 2, 1, 3)), bvectors, jnp.transpose(gshift, (2, 1, 0))
        )
    )
    dma = pltpu.SemaphoreType.DMA
    f32 = jnp.float32
    result = pl.pallas_call(
        kernel,
        out_shape=jax.ShapeDtypeStruct((4, 2, 32, 32), f32),
        in_specs=[
            pl.BlockSpec(memory_space=pltpu.HBM),
            pl.BlockSpec(memory_space=pltpu.HBM),
            pl.BlockSpec(memory_space=pltpu.HBM),
        ],
        out_specs=pl.BlockSpec(memory_space=pltpu.VMEM),
        scratch_shapes=[
            pltpu.SMEM((2, 3), f32),
            pltpu.SMEM((3, 2, 32), jnp.int32),
            pltpu.VMEM((SLOTS, 2, 3, 32, TILES * LANES), f32),
            pltpu.VMEM((SLOTS, 2, 32, LANES), f32),
            pltpu.VMEM((2, 16, (TILES + 1) * LANES), f32),
            pltpu.VMEM((ROW, 64, LANES), f32),
            pltpu.VMEM((SLOTS, 4, 16, LANES), f32),
            pltpu.VMEM((ROW, 4, 16, LANES), f32),
            pltpu.VMEM((4, 16, LANES), f32),
            pltpu.VMEM((4, 4, 16, LANES), f32),
            dma((2,)),
            dma,
            dma((len(EARLY),)),
            dma((len(LATE),)),
            dma((len(EARLY),)),
            dma,
            dma((3,)),
            dma((len(EARLY),)),
            dma,
            dma((SLOTS,)),
            dma,
            dma((3,)),
            dma,
            pltpu.SemaphoreType.REGULAR,
            pltpu.SemaphoreType.REGULAR((2,)),
        ],
        compiler_params=pltpu.CompilerParams(
            collective_id=0, has_side_effects=True, vmem_limit_bytes=40000 * 1024
        ),
        name="wannier",
    )(vectors, shifts, local)
    return result[None]


def solution(mesh):
    in_specs = (P("ka", None, None, None, "gz"), P(), P())
    out_specs = P("ka", None, None, None, None)
    return jax.shard_map(
        per_device, mesh=mesh, in_specs=in_specs, out_specs=out_specs, check_vma=False
    )
```

```python
import math

import jax
import jax.numpy as jnp
from jax import lax
from jax.experimental import pallas as pl
from jax.experimental.pallas import tpu as pltpu
from jax.sharding import PartitionSpec as P

GX = 40
GY = 40
NZ = 16
ROW = 8
ROWS = 4
SLOTS = 12
TILES = 6
LANES = 128
EARLY = ((0, 3), (3, 3))
LATE = ((0, 3), (3, 2), (5, 1))
MESH = pl.DeviceIdType.MESH
TWO_PI = 2.0 * math.pi


def split(value):
    high = value.astype(jnp.bfloat16)
    low = (value - high.astype(jnp.float32)).astype(jnp.bfloat16)
    return high, low


def contract(left, right):
    return lax.dot_general(
        left, right, (((1,), (1,)), ((), ())), preferred_element_type=jnp.float32
    )


def kernel(
    bvec_hbm, gshift_hbm, field_ref, out_ref,
    bvec_ref, gshift_ref, buf, xbuf, phase, acc, stage, reduced, total, gathered,
    small_sem, send_sem, early_sem, late_sem, passed_sem, xsend_sem, xrecv_sem, fsend_sem, xfsend_sem,
    rsend_sem, rrecv_sem, gsend_sem, grecv_sem, rows_sem, across_sem,
):
    me = lax.axis_index("ka")
    gx = lax.axis_index("gz")
    row = me // ROW
    own = me % ROW
    zpos = own // 2
    core = own % 2
    side = zpos // 2
    row_up = (row + 1) % ROWS
    row_down = (row + ROWS - 1) % ROWS
    pass_row = jnp.where(core == 0, row_down, row_up)
    pass_from = 8 * core
    pass_to = 8 - 8 * core
    first_k = row * ROW - 4 * core

    def at(r, j):
        return {"ka": r * ROW + j}

    sibling = zpos * 2 + 1 - core
    others = [((zpos + dz) % 4) * 2 for dz in (1, 3, 2)]
    barrier = pltpu.get_barrier_semaphore()
    near = [at(row, z + c) for z in others[:2] for c in range(2)] + [at(row, sibling)]
    near += [at(row_up, own), at(row_down, own)]
    near += [{"gz": (gx + 1) % 4}, {"gz": (gx + 3) % 4}]
    for device in near:
        pl.semaphore_signal(barrier, inc=1, device_id=device, device_id_type=MESH)
    small = [
        pltpu.make_async_copy(bvec_hbm, bvec_ref, small_sem.at[0]),
        pltpu.make_async_copy(gshift_hbm, gshift_ref, small_sem.at[1]),
    ]
    for copy in small:
        copy.start()

    pl.semaphore_wait(barrier, len(near))
    pl.semaphore_signal(across_sem.at[0], inc=1, device_id=at(row, others[1] + core), device_id_type=MESH)
    pl.semaphore_signal(across_sem.at[1], inc=1, device_id={"gz": (gx + 3) % 4}, device_id_type=MESH)

    def extra_source(p):
        comp = jnp.minimum(p // 2, 2)
        start = pl.multiple_of((ROW * TILES + p % 2) * LANES, LANES)
        return field_ref.at[:, comp, :, pl.ds(start, LANES)]

    def lanes_of(block):
        return pl.ds(block[0] * LANES, block[1] * LANES)

    def block_source(p, block):
        start = pl.multiple_of((p * TILES + block[0]) * LANES, LANES)
        return field_ref.at[:, :, :, pl.ds(start, block[1] * LANES)]

    def block_target(slot, block):
        return buf.at[slot, :, :, :, lanes_of(block)]

    def send_extra(z, c):
        pltpu.make_async_remote_copy(
            src_ref=extra_source(z + c), dst_ref=xbuf.at[own + 4 * c],
            send_sem=xsend_sem, recv_sem=xrecv_sem.at[side + c],
            device_id=at(row, z + c), device_id_type=MESH,
        ).start()

    def keep_extra(c):
        pltpu.make_async_copy(
            extra_source(own), xbuf.at[own + 4 * c], xrecv_sem.at[side + c]
        ).start()

    def send_blocks(z, c, blocks, sems):
        for n, block in blocks:
            pltpu.make_async_remote_copy(
                src_ref=block_source(z + c, block), dst_ref=block_target(own + 4 * c, block),
                send_sem=send_sem, recv_sem=sems.at[n],
                device_id=at(row, z + c), device_id_type=MESH,
            ).start()

    def keep_blocks(c, blocks, sems):
        for n, block in blocks:
            pltpu.make_async_copy(
                block_source(own, block), block_target(own + 4 * c, block), sems.at[n]
            ).start()

    early = list(enumerate(EARLY))
    late = list(enumerate(LATE))
    for z in others[:2]:
        send_extra(z, side)
    for z in others[:2]:
        send_blocks(z, side, early[:1], early_sem)
    pl.semaphore_wait(across_sem.at[0], 1)
    send_extra(others[2], side)
    send_blocks(others[2], side, early[:1], early_sem)
    for pair in early[1:]:
        for z in others:
            send_blocks(z, side, [pair], early_sem)
    here = zpos * 2

    @pl.when(core == side)
    def _():
        keep_extra(side)
        keep_blocks(side, early, early_sem)
        send_extra(here, 1 - side)
        send_blocks(here, 1 - side, late, late_sem)

    @pl.when(core != side)
    def _():
        send_extra(here, side)
        send_blocks(here, side, early, early_sem)
        keep_extra(1 - side)
        keep_blocks(1 - side, late, late_sem)

    for pair in late:
        for z in others:
            send_blocks(z, 1 - side, [pair], late_sem)
    for z in others:
        send_extra(z, 1 - side)

    for r in (row_up, row_down):
        pl.semaphore_signal(rows_sem, inc=1, device_id=at(r, own), device_id_type=MESH)

    for copy in small:
        copy.wait()

    row_id = lax.broadcasted_iota(jnp.int32, (16, LANES), 0)
    lane = lax.broadcasted_iota(jnp.int32, (16, TILES * LANES), 1).astype(jnp.float32)
    q = []
    for a in range(3):
        values = jnp.zeros((16, LANES), jnp.float32)
        for d in range(2):
            for i in range(8):
                k = (first_k + i + 32) % 32
                value = bvec_ref[d, a] + gshift_ref[a, d, k].astype(jnp.float32)
                values = jnp.where(row_id == d * 8 + i, value, values)
        q.append(jnp.concatenate([values] * TILES, axis=1))

    def phases_of(start, width):
        cell = lane[:, :width] + start.astype(jnp.float32)
        line = jnp.floor((cell + 0.5) * (1.0 / GX))
        plane = jnp.floor((cell + 0.5) * (1.0 / (GX * GY)))
        xc = cell - GX * line
        yc = line - GY * plane
        zc = plane + (gx * 4).astype(jnp.float32)
        q0, q1, q2 = (values[:, :width] for values in q)
        theta = -TWO_PI * (q0 * xc / GX + q1 * yc / GY + q2 * zc / NZ)
        return jnp.cos(theta), jnp.sin(theta)

    cosine, sine = phases_of(own * TILES * LANES, TILES * LANES)
    phase[0, :, pl.ds(0, TILES * LANES)] = cosine
    phase[1, :, pl.ds(0, TILES * LANES)] = sine
    cosine, sine = phases_of((ROW * TILES + own % 2) * LANES, LANES)
    keep = (own < 6).astype(jnp.float32)
    phase[0, :, pl.ds(TILES * LANES, LANES)] = cosine * keep
    phase[1, :, pl.ds(TILES * LANES, LANES)] = sine * keep
    acc[...] = jnp.zeros_like(acc)

    def wait_block(group, block, sem):
        target = block_target(pl.ds(4 * group, 4), block)
        pltpu.make_async_copy(target, target, sem).wait()

    def wait_extra(group):
        block = xbuf.at[pl.ds(4 * group, 4)]
        pltpu.make_async_copy(block, block, xrecv_sem.at[group]).wait()

    pass_extra = pltpu.make_async_remote_copy(
        src_ref=xbuf.at[pl.ds(pass_from, 4)], dst_ref=xbuf.at[pl.ds(pass_to, 4)],
        send_sem=xfsend_sem, recv_sem=xrecv_sem.at[2 - 2 * core],
        device_id=at(pass_row, own), device_id_type=MESH,
    )

    def pass_block(n, block):
        return pltpu.make_async_remote_copy(
            src_ref=block_target(pl.ds(pass_from, 4), block),
            dst_ref=block_target(pl.ds(pass_to, 4), block),
            send_sem=fsend_sem.at[n], recv_sem=passed_sem.at[n],
            device_id=at(pass_row, own), device_id_type=MESH,
        )

    wait_extra(2 * core)
    pass_extra.start()
    for n, block in early:
        wait_block(2 * core, block, early_sem.at[n])
        pass_block(n, block).start()

    def pair_products(left, rights):
        left_high, left_low = split(left)
        right_high, right_low = split(jnp.concatenate(rights, axis=0))
        both = contract(
            jnp.concatenate([left_high, left_low], axis=0),
            jnp.concatenate([right_high, right_low], axis=0),
        )
        return both[:64, :128] + both[64:, :128] + both[:64, 128:]

    def rotate(real, imag, lanes, d, i, comps):
        c = phase[0, pl.ds(d * 8 + i, 1), lanes]
        s = phase[1, pl.ds(d * 8 + i, 1), lanes]
        width = c.shape[1]
        c = jnp.concatenate([jnp.broadcast_to(c, (32, width))] * comps, axis=1)
        s = jnp.concatenate([jnp.broadcast_to(s, (32, width))] * comps, axis=1)
        return [c * real - s * imag, s * real + c * imag]

    def extra_step(i):
        left = xbuf[i].reshape(64, LANES)
        lanes = pl.ds(TILES * LANES, LANES)
        rights = []
        for d, offset in enumerate((1, 4)):
            rights += rotate(xbuf[i + offset, 0], xbuf[i + offset, 1], lanes, d, i, 1)
        acc[i] += pair_products(left, rights)

    def wide(slot, part, lanes):
        return jnp.concatenate([buf[slot, part, comp, :, lanes] for comp in range(3)], axis=1)

    def block_step(i, block):
        lanes = lanes_of(block)
        left = jnp.concatenate([wide(i, 0, lanes), wide(i, 1, lanes)], axis=0)
        rights = []
        for d, offset in enumerate((1, 4)):
            rights += rotate(wide(i + offset, 0, lanes), wide(i + offset, 1, lanes), lanes, d, i, 3)
        acc[i] += pair_products(left, rights)

    lane32 = lax.broadcasted_iota(jnp.int32, (32, LANES), 1)
    lane16 = lax.broadcasted_iota(jnp.int32, (16, LANES), 1)
    holder = core * 4 + zpos
    spans = [(0, 2)] + [(0, 3)] * 3 + [(0, 4)] * 4 + [(2, 2)] + [(3, 1)] * 3

    def target_copy(i):
        part = pl.ds(*spans[i])
        target = (first_k + i + 32) % 32
        return target, pltpu.make_async_remote_copy(
            src_ref=stage.at[i, part], dst_ref=reduced.at[holder, part],
            send_sem=rsend_sem.at[i], recv_sem=rrecv_sem,
            device_id={"ka": target}, device_id_type=MESH,
        )

    def send_target(i):
        part = pl.ds(*spans[i])
        target, copy = target_copy(i)

        def stay():
            pltpu.make_async_copy(stage.at[i, part], reduced.at[holder, part], rrecv_sem).start()

        lax.cond(target == me, stay, copy.start)

    def finish_matrices(i):
        top = acc[i, pl.ds(0, 32), :]
        bottom = acc[i, pl.ds(32, 32), :]
        swapped = jnp.where(
            lane32 % 64 < 32, pltpu.roll(bottom, 96, 1), -pltpu.roll(bottom, 32, 1)
        )
        value = top + swapped
        turned = pltpu.roll(value, 64, 1)
        along_x = jnp.where(lane16 < 64, value[:16], turned[16:])
        along_y = jnp.where(lane16 < 64, turned[:16], value[16:])
        stage[i, 0] = along_x
        stage[i, 1] = along_y
        stage[i + 1, 2] = along_x
        stage[i + 4, 3] = along_y

    for n, block in late:
        for e, other in early:
            if block[0] <= other[0] < block[0] + block[1]:
                wait_block(2 - 2 * core, other, passed_sem.at[e])
        wait_block(1, block, late_sem.at[n])
        for i in range(ROW):
            block_step(i, block)
    pl.semaphore_wait(across_sem.at[1], 1)
    pl.semaphore_wait(rows_sem, 2)
    wait_extra(2 - 2 * core)
    wait_extra(1)
    for i in range(ROW):
        extra_step(i)
        finish_matrices(i)
    for i in range(SLOTS):
        send_target(i)

    def slab_copy(dx):
        return pltpu.make_async_remote_copy(
            src_ref=total, dst_ref=gathered.at[gx],
            send_sem=gsend_sem.at[dx - 1], recv_sem=grecv_sem,
            device_id={"gz": (gx + dx) % 4}, device_id_type=MESH,
        )

    pltpu.make_async_copy(reduced, reduced, rrecv_sem).wait()
    value = reduced[0]
    for j in range(1, ROW):
        value = value + reduced[j]
    total[...] = value
    for dx in (2, 1, 3):
        slab_copy(dx).start()
    gathered[gx] = value

    seven = xbuf.at[pl.ds(0, 7)]
    pltpu.make_async_copy(seven, seven, xsend_sem).wait()
    pass_extra.wait_send()

    sent = buf.at[pl.ds(0, 7)]
    pltpu.make_async_copy(sent, sent, send_sem).wait()
    for n, block in early:
        pass_block(n, block).wait_send()
    for i in range(SLOTS):
        target, copy = target_copy(i)

        @pl.when(target != me)
        def _():
            copy.wait_send()

    block = gathered.at[pl.ds(0, 3)]
    pltpu.make_async_copy(block, block, grecv_sem).wait()
    summed = gathered[0] + gathered[1] + gathered[2] + gathered[3]
    for index, direction in ((0, 0), (1, 2), (2, 1), (3, 3)):
        value = summed[index]
        real = jnp.concatenate([value[:, 0:32], value[:, 64:96]], axis=0)
        imag = jnp.concatenate([value[:, 32:64], value[:, 96:128]], axis=0)
        if index < 2:
            out_ref[direction, 0] = real
            out_ref[direction, 1] = imag
        else:
            out_ref[direction, 0] = real.T
            out_ref[direction, 1] = -imag.T
    for dx in (1, 2, 3):
        slab_copy(dx).wait_send()


def per_device(fields, bvectors, gshift):
    local, vectors, shifts = (
        pltpu.with_memory_space_constraint(value, pltpu.HBM)
        for value in (
            jnp.transpose(fields[0], (0, 2, 1, 3)), bvectors, jnp.transpose(gshift, (2, 1, 0))
        )
    )
    dma = pltpu.SemaphoreType.DMA
    f32 = jnp.float32
    result = pl.pallas_call(
        kernel,
        out_shape=jax.ShapeDtypeStruct((4, 2, 32, 32), f32),
        in_specs=[
            pl.BlockSpec(memory_space=pltpu.HBM),
            pl.BlockSpec(memory_space=pltpu.HBM),
            pl.BlockSpec(memory_space=pltpu.HBM),
        ],
        out_specs=pl.BlockSpec(memory_space=pltpu.VMEM),
        scratch_shapes=[
            pltpu.SMEM((2, 3), f32),
            pltpu.SMEM((3, 2, 32), jnp.int32),
            pltpu.VMEM((SLOTS, 2, 3, 32, TILES * LANES), f32),
            pltpu.VMEM((SLOTS, 2, 32, LANES), f32),
            pltpu.VMEM((2, 16, (TILES + 1) * LANES), f32),
            pltpu.VMEM((ROW, 64, LANES), f32),
            pltpu.VMEM((SLOTS, 4, 16, LANES), f32),
            pltpu.VMEM((ROW, 4, 16, LANES), f32),
            pltpu.VMEM((4, 16, LANES), f32),
            pltpu.VMEM((4, 4, 16, LANES), f32),
            dma((2,)),
            dma,
            dma((len(EARLY),)),
            dma((len(LATE),)),
            dma((len(EARLY),)),
            dma,
            dma((3,)),
            dma((len(EARLY),)),
            dma,
            dma((SLOTS,)),
            dma,
            dma((3,)),
            dma,
            pltpu.SemaphoreType.REGULAR,
            pltpu.SemaphoreType.REGULAR((2,)),
        ],
        compiler_params=pltpu.CompilerParams(
            collective_id=0, has_side_effects=True, vmem_limit_bytes=40000 * 1024
        ),
        name="wannier",
    )(vectors, shifts, local)
    return result[None]


def solution(mesh):
    in_specs = (P("ka", None, None, None, "gz"), P(), P())
    out_specs = P("ka", None, None, None, None)
    return jax.shard_map(
        per_device, mesh=mesh, in_specs=in_specs, out_specs=out_specs, check_vma=False
    )
```

```python
import math

import jax
import jax.numpy as jnp
from jax import lax
from jax.experimental import pallas as pl
from jax.experimental.pallas import tpu as pltpu
from jax.sharding import PartitionSpec as P

GX = 40
GY = 40
NZ = 16
ROW = 8
ROWS = 4
SLOTS = 12
TILES = 6
LANES = 128
EARLY = ((0, 3), (3, 3))
LATE = ((0, 3), (3, 2), (5, 1))
MESH = pl.DeviceIdType.MESH
TWO_PI = 2.0 * math.pi


def split(value):
    high = value.astype(jnp.bfloat16)
    low = (value - high.astype(jnp.float32)).astype(jnp.bfloat16)
    return high, low


def contract(left, right):
    return lax.dot_general(
        left, right, (((1,), (1,)), ((), ())), preferred_element_type=jnp.float32
    )


def kernel(
    bvec_hbm, gshift_hbm, field_ref, out_ref,
    bvec_ref, gshift_ref, buf, xbuf, phase, acc, stage, reduced, total, gathered,
    small_sem, send_sem, early_sem, late_sem, passed_sem, xsend_sem, xrecv_sem, fsend_sem, xfsend_sem,
    rsend_sem, rrecv_sem, gsend_sem, grecv_sem, rows_sem, across_sem,
):
    me = lax.axis_index("ka")
    gx = lax.axis_index("gz")
    row = me // ROW
    own = me % ROW
    zpos = own // 2
    core = own % 2
    side = zpos // 2
    row_up = (row + 1) % ROWS
    row_down = (row + ROWS - 1) % ROWS
    pass_row = jnp.where(core == 0, row_down, row_up)
    pass_from = 8 * core
    pass_to = 8 - 8 * core
    first_k = row * ROW - 4 * core

    def at(r, j):
        return {"ka": r * ROW + j}

    sibling = zpos * 2 + 1 - core
    others = [((zpos + dz) % 4) * 2 for dz in (1, 3, 2)]
    barrier = pltpu.get_barrier_semaphore()
    near = [at(row, z + c) for z in others[:2] for c in range(2)] + [at(row, sibling)]
    near += [at(row_up, own), at(row_down, own)]
    near += [{"gz": (gx + 1) % 4}, {"gz": (gx + 3) % 4}]
    for device in near:
        pl.semaphore_signal(barrier, inc=1, device_id=device, device_id_type=MESH)
    small = [
        pltpu.make_async_copy(bvec_hbm, bvec_ref, small_sem.at[0]),
        pltpu.make_async_copy(gshift_hbm, gshift_ref, small_sem.at[1]),
    ]
    for copy in small:
        copy.start()

    pl.semaphore_wait(barrier, len(near))
    pl.semaphore_signal(across_sem.at[0], inc=1, device_id=at(row, others[1] + core), device_id_type=MESH)
    pl.semaphore_signal(across_sem.at[1], inc=1, device_id={"gz": (gx + 3) % 4}, device_id_type=MESH)

    def extra_source(p):
        comp = jnp.minimum(p // 2, 2)
        start = pl.multiple_of((ROW * TILES + p % 2) * LANES, LANES)
        return field_ref.at[:, comp, :, pl.ds(start, LANES)]

    def lanes_of(block):
        return pl.ds(block[0] * LANES, block[1] * LANES)

    def block_source(p, block):
        start = pl.multiple_of((p * TILES + block[0]) * LANES, LANES)
        return field_ref.at[:, :, :, pl.ds(start, block[1] * LANES)]

    def block_target(slot, block):
        return buf.at[slot, :, :, :, lanes_of(block)]

    def send_extra(z, c):
        pltpu.make_async_remote_copy(
            src_ref=extra_source(z + c), dst_ref=xbuf.at[own + 4 * c],
            send_sem=xsend_sem, recv_sem=xrecv_sem.at[side + c],
            device_id=at(row, z + c), device_id_type=MESH,
        ).start()

    def keep_extra(c):
        pltpu.make_async_copy(
            extra_source(own), xbuf.at[own + 4 * c], xrecv_sem.at[side + c]
        ).start()

    def send_blocks(z, c, blocks, sems):
        for n, block in blocks:
            pltpu.make_async_remote_copy(
                src_ref=block_source(z + c, block), dst_ref=block_target(own + 4 * c, block),
                send_sem=send_sem, recv_sem=sems.at[n],
                device_id=at(row, z + c), device_id_type=MESH,
            ).start()

    def keep_blocks(c, blocks, sems):
        for n, block in blocks:
            pltpu.make_async_copy(
                block_source(own, block), block_target(own + 4 * c, block), sems.at[n]
            ).start()

    early = list(enumerate(EARLY))
    late = list(enumerate(LATE))
    for z in others[:2]:
        send_extra(z, side)
    for z in others[:2]:
        send_blocks(z, side, early[:1], early_sem)
    pl.semaphore_wait(across_sem.at[0], 1)
    send_extra(others[2], side)
    send_blocks(others[2], side, early[:1], early_sem)
    for pair in early[1:]:
        for z in others:
            send_blocks(z, side, [pair], early_sem)
    here = zpos * 2

    @pl.when(core == side)
    def _():
        keep_extra(side)
        keep_blocks(side, early, early_sem)
        send_extra(here, 1 - side)
        send_blocks(here, 1 - side, late, late_sem)

    @pl.when(core != side)
    def _():
        send_extra(here, side)
        send_blocks(here, side, early, early_sem)
        keep_extra(1 - side)
        keep_blocks(1 - side, late, late_sem)

    for pair in late:
        for z in others:
            send_blocks(z, 1 - side, [pair], late_sem)
    for z in others:
        send_extra(z, 1 - side)

    for r in (row_up, row_down):
        pl.semaphore_signal(rows_sem, inc=1, device_id=at(r, own), device_id_type=MESH)

    for copy in small:
        copy.wait()

    row_id = lax.broadcasted_iota(jnp.int32, (16, LANES), 0)
    lane = lax.broadcasted_iota(jnp.int32, (16, TILES * LANES), 1).astype(jnp.float32)
    q = []
    for a in range(3):
        values = jnp.zeros((16, LANES), jnp.float32)
        for d in range(2):
            for i in range(8):
                k = (first_k + i + 32) % 32
                value = bvec_ref[d, a] + gshift_ref[a, d, k].astype(jnp.float32)
                values = jnp.where(row_id == d * 8 + i, value, values)
        q.append(jnp.concatenate([values] * TILES, axis=1))

    def phases_of(start, width):
        cell = lane[:, :width] + start.astype(jnp.float32)
        line = jnp.floor((cell + 0.5) * (1.0 / GX))
        plane = jnp.floor((cell + 0.5) * (1.0 / (GX * GY)))
        xc = cell - GX * line
        yc = line - GY * plane
        zc = plane + (gx * 4).astype(jnp.float32)
        q0, q1, q2 = (values[:, :width] for values in q)
        theta = -TWO_PI * (q0 * xc / GX + q1 * yc / GY + q2 * zc / NZ)
        return jnp.cos(theta), jnp.sin(theta)

    cosine, sine = phases_of(own * TILES * LANES, TILES * LANES)
    phase[0, :, pl.ds(0, TILES * LANES)] = cosine
    phase[1, :, pl.ds(0, TILES * LANES)] = sine
    cosine, sine = phases_of((ROW * TILES + own % 2) * LANES, LANES)
    keep = (own < 6).astype(jnp.float32)
    phase[0, :, pl.ds(TILES * LANES, LANES)] = cosine * keep
    phase[1, :, pl.ds(TILES * LANES, LANES)] = sine * keep
    acc[...] = jnp.zeros_like(acc)

    def wait_block(group, block, sem):
        target = block_target(pl.ds(4 * group, 4), block)
        pltpu.make_async_copy(target, target, sem).wait()

    def wait_extra(group):
        block = xbuf.at[pl.ds(4 * group, 4)]
        pltpu.make_async_copy(block, block, xrecv_sem.at[group]).wait()

    pass_extra = pltpu.make_async_remote_copy(
        src_ref=xbuf.at[pl.ds(pass_from, 4)], dst_ref=xbuf.at[pl.ds(pass_to, 4)],
        send_sem=xfsend_sem, recv_sem=xrecv_sem.at[2 - 2 * core],
        device_id=at(pass_row, own), device_id_type=MESH,
    )

    def pass_block(n, block):
        return pltpu.make_async_remote_copy(
            src_ref=block_target(pl.ds(pass_from, 4), block),
            dst_ref=block_target(pl.ds(pass_to, 4), block),
            send_sem=fsend_sem.at[n], recv_sem=passed_sem.at[n],
            device_id=at(pass_row, own), device_id_type=MESH,
        )

    wait_extra(2 * core)
    pass_extra.start()
    for n, block in early:
        wait_block(2 * core, block, early_sem.at[n])
        pass_block(n, block).start()

    def pair_products(left, rights):
        left_high, left_low = split(left)
        right_high, right_low = split(jnp.concatenate(rights, axis=0))
        both = contract(
            jnp.concatenate([left_high, left_low], axis=0),
            jnp.concatenate([right_high, right_low], axis=0),
        )
        return both[:64, :128] + both[64:, :128] + both[:64, 128:]

    def rotate(real, imag, lanes, d, i, comps):
        c = phase[0, pl.ds(d * 8 + i, 1), lanes]
        s = phase[1, pl.ds(d * 8 + i, 1), lanes]
        width = c.shape[1]
        c = jnp.concatenate([jnp.broadcast_to(c, (32, width))] * comps, axis=1)
        s = jnp.concatenate([jnp.broadcast_to(s, (32, width))] * comps, axis=1)
        return [c * real - s * imag, s * real + c * imag]

    def extra_step(i):
        left = xbuf[i].reshape(64, LANES)
        lanes = pl.ds(TILES * LANES, LANES)
        rights = []
        for d, offset in enumerate((1, 4)):
            rights += rotate(xbuf[i + offset, 0], xbuf[i + offset, 1], lanes, d, i, 1)
        return pair_products(left, rights)

    def wide(slot, part, lanes):
        return jnp.concatenate([buf[slot, part, comp, :, lanes] for comp in range(3)], axis=1)

    def block_step(i, block):
        lanes = lanes_of(block)
        left = jnp.concatenate([wide(i, 0, lanes), wide(i, 1, lanes)], axis=0)
        rights = []
        for d, offset in enumerate((1, 4)):
            rights += rotate(wide(i + offset, 0, lanes), wide(i + offset, 1, lanes), lanes, d, i, 3)
        acc[i] += pair_products(left, rights)

    lane32 = lax.broadcasted_iota(jnp.int32, (32, LANES), 1)
    lane16 = lax.broadcasted_iota(jnp.int32, (16, LANES), 1)
    holder = core * 4 + zpos
    spans = [(0, 2)] + [(0, 3)] * 3 + [(0, 4)] * 4 + [(2, 2)] + [(3, 1)] * 3

    def target_copy(i):
        part = pl.ds(*spans[i])
        target = (first_k + i + 32) % 32
        return target, pltpu.make_async_remote_copy(
            src_ref=stage.at[i, part], dst_ref=reduced.at[holder, part],
            send_sem=rsend_sem.at[i], recv_sem=rrecv_sem,
            device_id={"ka": target}, device_id_type=MESH,
        )

    def send_target(i):
        part = pl.ds(*spans[i])
        target, copy = target_copy(i)

        def stay():
            pltpu.make_async_copy(stage.at[i, part], reduced.at[holder, part], rrecv_sem).start()

        lax.cond(target == me, stay, copy.start)

    def finish_matrices(i, products):
        top, bottom = products[:32], products[32:]
        swapped = jnp.where(
            lane32 % 64 < 32, pltpu.roll(bottom, 96, 1), -pltpu.roll(bottom, 32, 1)
        )
        value = top + swapped
        turned = pltpu.roll(value, 64, 1)
        along_x = jnp.where(lane16 < 64, value[:16], turned[16:])
        along_y = jnp.where(lane16 < 64, turned[:16], value[16:])
        stage[i, 0] = along_x
        stage[i, 1] = along_y
        stage[i + 1, 2] = along_x
        stage[i + 4, 3] = along_y

    for n, block in late:
        for e, other in early:
            if block[0] <= other[0] < block[0] + block[1]:
                wait_block(2 - 2 * core, other, passed_sem.at[e])
        wait_block(1, block, late_sem.at[n])
        for i in range(ROW):
            block_step(i, block)
    pl.semaphore_wait(across_sem.at[1], 1)
    pl.semaphore_wait(rows_sem, 2)
    wait_extra(2 - 2 * core)
    wait_extra(1)
    for i in range(ROW):
        finish_matrices(i, acc[i] + extra_step(i))
    for i in range(SLOTS):
        send_target(i)

    def slab_copy(dx):
        return pltpu.make_async_remote_copy(
            src_ref=total, dst_ref=gathered.at[gx],
            send_sem=gsend_sem.at[dx - 1], recv_sem=grecv_sem,
            device_id={"gz": (gx + dx) % 4}, device_id_type=MESH,
        )

    pltpu.make_async_copy(reduced, reduced, rrecv_sem).wait()
    value = reduced[0]
    for j in range(1, ROW):
        value = value + reduced[j]
    total[...] = value
    for dx in (2, 1, 3):
        slab_copy(dx).start()
    gathered[gx] = value

    seven = xbuf.at[pl.ds(0, 7)]
    pltpu.make_async_copy(seven, seven, xsend_sem).wait()
    pass_extra.wait_send()

    sent = buf.at[pl.ds(0, 7)]
    pltpu.make_async_copy(sent, sent, send_sem).wait()
    for n, block in early:
        pass_block(n, block).wait_send()
    for i in range(SLOTS):
        target, copy = target_copy(i)

        @pl.when(target != me)
        def _():
            copy.wait_send()

    block = gathered.at[pl.ds(0, 3)]
    pltpu.make_async_copy(block, block, grecv_sem).wait()
    summed = gathered[0] + gathered[1] + gathered[2] + gathered[3]
    for index, direction in ((0, 0), (1, 2), (2, 1), (3, 3)):
        value = summed[index]
        real = jnp.concatenate([value[:, 0:32], value[:, 64:96]], axis=0)
        imag = jnp.concatenate([value[:, 32:64], value[:, 96:128]], axis=0)
        if index < 2:
            out_ref[direction, 0] = real
            out_ref[direction, 1] = imag
        else:
            out_ref[direction, 0] = real.T
            out_ref[direction, 1] = -imag.T
    for dx in (1, 2, 3):
        slab_copy(dx).wait_send()


def per_device(fields, bvectors, gshift):
    local, vectors, shifts = (
        pltpu.with_memory_space_constraint(value, pltpu.HBM)
        for value in (
            jnp.transpose(fields[0], (0, 2, 1, 3)), bvectors, jnp.transpose(gshift, (2, 1, 0))
        )
    )
    dma = pltpu.SemaphoreType.DMA
    f32 = jnp.float32
    result = pl.pallas_call(
        kernel,
        out_shape=jax.ShapeDtypeStruct((4, 2, 32, 32), f32),
        in_specs=[
            pl.BlockSpec(memory_space=pltpu.HBM),
            pl.BlockSpec(memory_space=pltpu.HBM),
            pl.BlockSpec(memory_space=pltpu.HBM),
        ],
        out_specs=pl.BlockSpec(memory_space=pltpu.VMEM),
        scratch_shapes=[
            pltpu.SMEM((2, 3), f32),
            pltpu.SMEM((3, 2, 32), jnp.int32),
            pltpu.VMEM((SLOTS, 2, 3, 32, TILES * LANES), f32),
            pltpu.VMEM((SLOTS, 2, 32, LANES), f32),
            pltpu.VMEM((2, 16, (TILES + 1) * LANES), f32),
            pltpu.VMEM((ROW, 64, LANES), f32),
            pltpu.VMEM((SLOTS, 4, 16, LANES), f32),
            pltpu.VMEM((ROW, 4, 16, LANES), f32),
            pltpu.VMEM((4, 16, LANES), f32),
            pltpu.VMEM((4, 4, 16, LANES), f32),
            dma((2,)),
            dma,
            dma((len(EARLY),)),
            dma((len(LATE),)),
            dma((len(EARLY),)),
            dma,
            dma((3,)),
            dma((len(EARLY),)),
            dma,
            dma((SLOTS,)),
            dma,
            dma((3,)),
            dma,
            pltpu.SemaphoreType.REGULAR,
            pltpu.SemaphoreType.REGULAR((2,)),
        ],
        compiler_params=pltpu.CompilerParams(
            collective_id=0, has_side_effects=True, vmem_limit_bytes=40000 * 1024
        ),
        name="wannier",
    )(vectors, shifts, local)
    return result[None]


def solution(mesh):
    in_specs = (P("ka", None, None, None, "gz"), P(), P())
    out_specs = P("ka", None, None, None, None)
    return jax.shard_map(
        per_device, mesh=mesh, in_specs=in_specs, out_specs=out_specs, check_vma=False
    )
```
